32 devices in a mesh: tile: 16 (over z, x, core), probe: 2 (over y).
Axes of the slice: x: 2, y: 2, z: 4, core: 2. Of those that a mesh axis runs over, the one named last changes fastest.
Arguments:
- latent: float32 [16, 16, 4, 320], P(None, 'tile'), may hold values from -60 to 60, as said below
- probes: bfloat16 [2, 16, 16, 16, 4, 320], P(None, 'probe', None, 'tile'), may hold values from -60 to 60, as said below
- gn_gain: float32 [320], replicated, may hold values from 0.1 to 1.9
- gn_bias: float32 [320], replicated, may hold values from -3 to 3
- w_spatial: bfloat16 [9, 320, 320], replicated, may hold values from -0.109375 to 0.109375
- spatial_bias: float32 [320], replicated, may hold values from -3 to 3
- w_temporal: bfloat16 [3, 320, 320], replicated, may hold values from -0.1875 to 0.1875
- temporal_bias: float32 [320], replicated, may hold values from -3 to 3
- w_qkv: bfloat16 [320, 3, 320], replicated, may hold values from -0.3125 to 0.3125
- w_out: bfloat16 [320, 320], replicated, may hold values from -0.3125 to 0.3125
- temper: float32 [8], replicated, may hold values from 1 to 4
Outputs:
- block_out: bfloat16 [16, 16, 4, 320], P(None, 'tile')
- basis: float32 [16, 16, 16, 4, 320], P('probe', None, 'tile')
- basis_images: bfloat16 [16, 16, 16, 4, 320], P('probe', None, 'tile')
- test_images: bfloat16 [16, 16, 16, 4, 320], P('probe', None, 'tile')
- rayleigh: float32 [2, 16], replicated
- divergence: float32 [], replicated
The draws below stay inside these ranges and needn't reach their ends.
Inputs may be any that keep to these rules, and one draw needn't show every extreme that they name: `latent`: every element is drawn within the bounds. `probes`: every element is drawn within the bounds.
All inputs are finite; a program needn't handle non-finite values.
Results may differ from the reference program's by a relative error of at most 0.012.
Values may be sent and summed in bfloat16 or wider, within the bound.
A program may use at most 128 MiB of HBM per device.

```python
import math
import jax
import jax.numpy as jnp
from jax import lax

C = 320
GROUPS = 32
HEADS = 8
HEAD_DIM = 40
FRAMES = 16
COLS = 4
NS = 16
H = 16


def draw_latent(key, part):
    keys = jax.random.split(jax.random.fold_in(key, 11), 3)
    shape = (FRAMES, H, COLS, C)
    cell_scale = jnp.exp(jax.random.uniform(keys[0], (FRAMES, H, COLS, 1), jnp.float32, math.log(0.4), math.log(2.5)))
    channel_scale = jnp.exp(jax.random.uniform(keys[1], (C,), jnp.float32, math.log(0.5), math.log(2.0)))
    ramp = jnp.power(3.0, jnp.arange(H, dtype=jnp.float32) / max(H - 1, 1)).reshape(1, H, 1, 1)
    base = jnp.clip(jax.random.normal(keys[2], shape, jnp.float32), -4.0, 4.0)
    return (base * cell_scale * channel_scale * ramp).astype(jnp.float32)


def probe_noise(noise_key, shape):
    return jnp.clip(jax.random.normal(noise_key, shape, jnp.float32), -4.0, 4.0)


def draw_probes(key, part):
    keys = jax.random.split(jax.random.fold_in(key, 23), 4)
    shape = (NS, FRAMES, H, COLS, C)
    growth = 8.0
    ramp = jnp.power(growth, jnp.arange(H, dtype=jnp.float32) / max(H - 1, 1)).reshape(1, 1, H, 1, 1)
    magnitude = jax.random.uniform(keys[0], (2, NS, 1, 1, 1, C), jnp.float32, 0.5, 1.2)
    signs = jnp.where(jax.random.bernoulli(keys[1], 0.5, (2, NS, 1, 1, 1, C)), 1.0, -1.0)
    offsets = magnitude * signs
    sketch = probe_noise(keys[2], shape) + offsets[0]
    fresh = probe_noise(keys[3], shape) + offsets[1]
    test = 0.8 * sketch + 0.6 * fresh
    return (jnp.stack([sketch, test]) * ramp[None]).astype(jnp.bfloat16)


def gaussian(rng, dims, scale, limit, kind=jnp.bfloat16):
    return jnp.clip(scale * jax.random.normal(rng, dims, jnp.float32), -limit, limit).astype(kind)


def setup_inputs(seed: int = 0) -> dict:
    key_list = jax.random.split(jax.random.key(seed), 12)
    latent = draw_latent(jax.random.fold_in(key_list[11], 71), 0)
    probes = draw_probes(jax.random.fold_in(key_list[11], 71), 0)
    gn_gain = jnp.clip(1.0 + 0.18 * jax.random.normal(key_list[2], (C,), jnp.float32), 0.1, 1.9)
    gn_bias = gaussian(key_list[3], (C,), 0.5, 3.0, jnp.float32)
    w_spatial = gaussian(key_list[4], (9, C, C), (9 * C) ** -0.5, 0.109375)
    spatial_bias = gaussian(key_list[5], (C,), 0.5, 3.0, jnp.float32)
    w_temporal = gaussian(key_list[6], (3, C, C), (3 * C) ** -0.5, 0.1875)
    temporal_bias = gaussian(key_list[7], (C,), 0.5, 3.0, jnp.float32)
    w_qkv = gaussian(key_list[8], (C, 3, C), C ** -0.5, 0.3125)
    w_out = gaussian(key_list[9], (C, C), C ** -0.5, 0.3125)
    temper = jnp.clip(jnp.exp(jax.random.uniform(key_list[10], (HEADS,), jnp.float32, math.log(1.0), math.log(4.0))), 1.0, 4.0)
    return dict(latent=latent, probes=probes, gn_gain=gn_gain, gn_bias=gn_bias, w_spatial=w_spatial, spatial_bias=spatial_bias, w_temporal=w_temporal, temporal_bias=temporal_bias, w_qkv=w_qkv, w_out=w_out, temper=temper)


EPS = 1e-05
HIGHEST = lax.Precision.HIGHEST

def spread_groups(stat):
    return jnp.repeat(stat, C // GROUPS, axis=-1)

def row_conv(signal, w_spatial):
    padded = jnp.pad(signal, ((0, 0), (0, 0), (1, 1), (1, 1), (0, 0)))
    height = signal.shape[2]
    across = signal.shape[3]
    pieces = [padded[:, :, row_shift:row_shift + height, column_shift:column_shift + across, :] for row_shift in range(3) for column_shift in range(3)]
    stacked = jnp.concatenate(pieces, axis=-1)
    result = jnp.dot(stacked.reshape(-1, 9 * C).astype(jnp.float32), w_spatial.reshape(9 * C, C).astype(jnp.float32), preferred_element_type=jnp.float32)
    return result.reshape(signal.shape)

def frame_conv(signal, w_temporal):
    padded = jnp.pad(signal, ((0, 0), (1, 1), (0, 0), (0, 0), (0, 0)))
    frames = signal.shape[1]
    pieces = [padded[:, frame_shift:frame_shift + frames] for frame_shift in range(3)]
    stacked = jnp.concatenate(pieces, axis=-1)
    result = jnp.dot(stacked.reshape(-1, 3 * C).astype(jnp.float32), w_temporal.reshape(3 * C, C).astype(jnp.float32), preferred_element_type=jnp.float32)
    return result.reshape(signal.shape)

def project_heads(signal, w_qkv):
    flattened = jnp.dot(signal.reshape(-1, C).astype(jnp.float32), w_qkv.reshape(C, 3 * C).astype(jnp.float32), preferred_element_type=jnp.float32)
    return flattened.reshape(signal.shape[:-1] + (3, HEADS, HEAD_DIM))

def output_proj(mixture, shape, w_out):
    rounded = mixture.reshape(shape).astype(jnp.bfloat16)
    return jnp.dot(rounded.reshape(-1, C).astype(jnp.float32), w_out.astype(jnp.float32), preferred_element_type=jnp.float32).reshape(shape)

def lower_inverse(lower):
    order = lower.shape[0]
    inverse = jnp.zeros_like(lower)
    identity = jnp.eye(order, dtype=lower.dtype)
    for row in range(order):
        partial_row = identity[row] - jnp.dot(lower[row], inverse, precision=HIGHEST)
        inverse = inverse.at[row].set(partial_row / lower[row, row])
    return inverse

def primal_pass(latent, gn_gain, gn_bias, spatial_bias, temporal_bias, temper, filters):
    w_spatial, w_temporal, w_qkv, w_out = filters
    grouped = latent.reshape(-1, GROUPS, C // GROUPS)
    members = grouped.shape[0] * grouped.shape[2]
    totals = lax.optimization_barrier(jnp.sum(grouped, axis=(0, 2)))
    squares = lax.optimization_barrier(jnp.sum(grouped * grouped, axis=(0, 2)))
    group_mean = totals / members
    inv_std = lax.rsqrt(squares / members - group_mean * group_mean + EPS)
    centered = latent - spread_groups(group_mean)
    normed = centered * spread_groups(inv_std) * gn_gain + gn_bias
    gate_sigmoid = jax.nn.sigmoid(normed)
    sigmoid_slope = gate_sigmoid * (1.0 + normed * (1.0 - gate_sigmoid))
    active = (normed * gate_sigmoid).astype(jnp.bfloat16)
    spatial = row_conv(active[None], w_spatial)[0] + spatial_bias
    temporal = frame_conv(spatial.astype(jnp.bfloat16)[None], w_temporal)[0] + temporal_bias
    residual_sum = latent + temporal
    projected_qkv = project_heads(residual_sum.astype(jnp.bfloat16), w_qkv)
    queries = projected_qkv[..., 0, :, :]
    keys_all = projected_qkv[..., 1, :, :]
    values = projected_qkv[..., 2, :, :]
    query_norm = jnp.sqrt(lax.optimization_barrier(jnp.mean(queries * queries, axis=-1, keepdims=True)) + 1.0)
    key_norm = jnp.sqrt(lax.optimization_barrier(jnp.mean(keys_all * keys_all, axis=-1, keepdims=True)) + 1.0)
    query_unit = queries / query_norm
    key_unit = keys_all / key_norm
    factor = temper[:, None, None] / math.sqrt(HEAD_DIM)
    scores = jnp.einsum('fhwnd,ghwnd->hwnfg', query_unit, key_unit, precision=HIGHEST) * factor
    exponent = jnp.exp(scores)
    weights_soft = exponent / lax.optimization_barrier(jnp.sum(exponent, axis=-1, keepdims=True))
    mixture = jnp.einsum('hwnfg,ghwnd->fhwnd', weights_soft, values, precision=HIGHEST)
    output = residual_sum + output_proj(mixture, residual_sum.shape, w_out)
    cache = (centered, inv_std, sigmoid_slope, queries, keys_all, values, query_norm, key_norm, query_unit, key_unit, weights_soft)
    return (output.astype(jnp.bfloat16), cache)

def tangent_pass(tangents, cache, filters, gn_gain, temper):
    centered, inv_std, sigmoid_slope, queries, keys_all, values, query_norm, key_norm, query_unit, key_unit, weights_soft = cache
    w_spatial, w_temporal, w_qkv, w_out = filters
    batch = tangents.shape[0]
    grouped = tangents.reshape(batch, -1, GROUPS, C // GROUPS)
    members = grouped.shape[1] * grouped.shape[3]
    centered_groups = centered.reshape(1, -1, GROUPS, C // GROUPS)
    first = lax.optimization_barrier(jnp.sum(grouped, axis=(1, 3)))
    cross = lax.optimization_barrier(jnp.sum(grouped * centered_groups, axis=(1, 3)))
    shift_mean = first / members
    shift_var = 2.0 * cross / members
    shift_std = -0.5 * inv_std ** 3 * shift_var
    shifted_norm = ((tangents - spread_groups(shift_mean)[:, None, None, None, :]) * spread_groups(inv_std) + centered * spread_groups(shift_std)[:, None, None, None, :]) * gn_gain
    shifted_active = (sigmoid_slope * shifted_norm).astype(jnp.bfloat16)
    shifted_spatial = row_conv(shifted_active, w_spatial)
    shifted_temporal = frame_conv(shifted_spatial.astype(jnp.bfloat16), w_temporal)
    shifted_residual = tangents + shifted_temporal
    shifted_qkv = project_heads(shifted_residual.astype(jnp.bfloat16), w_qkv)
    query_shift = shifted_qkv[..., 0, :, :]
    key_shift = shifted_qkv[..., 1, :, :]
    value_shift = shifted_qkv[..., 2, :, :]
    query_unit_shift = query_shift / query_norm - queries * lax.optimization_barrier(jnp.mean(queries * query_shift, axis=-1, keepdims=True)) / query_norm ** 3
    key_unit_shift = key_shift / key_norm - keys_all * lax.optimization_barrier(jnp.mean(keys_all * key_shift, axis=-1, keepdims=True)) / key_norm ** 3
    factor = temper[:, None, None] / math.sqrt(HEAD_DIM)
    score_shift = (jnp.einsum('...fhwnd,...ghwnd->...hwnfg', query_unit_shift, key_unit, precision=HIGHEST) + jnp.einsum('...fhwnd,...ghwnd->...hwnfg', query_unit, key_unit_shift, precision=HIGHEST)) * factor
    weight_shift = weights_soft * (score_shift - lax.optimization_barrier(jnp.sum(weights_soft * score_shift, axis=-1, keepdims=True)))
    mixture_shift = jnp.einsum('...hwnfg,...ghwnd->...fhwnd', weight_shift, values, precision=HIGHEST) + jnp.einsum('...hwnfg,...ghwnd->...fhwnd', weights_soft, value_shift, precision=HIGHEST)
    return shifted_residual + output_proj(mixture_shift, shifted_residual.shape, w_out)

def reference(latent, probes, gn_gain, gn_bias, w_spatial, spatial_bias, w_temporal, temporal_bias, w_qkv, w_out, temper):
    filters = (w_spatial, w_temporal, w_qkv, w_out)
    block_out, cache = primal_pass(latent, gn_gain, gn_bias, spatial_bias, temporal_bias, temper, filters)
    total = latent.size

    def single_image(tangent):
        return tangent_pass(tangent[None], cache, filters, gn_gain, temper)[0]
    sketch_images = lax.map(single_image, probes[0].astype(jnp.float32))
    flattened = sketch_images.reshape(NS, -1)
    gram = jnp.dot(flattened, flattened.T, precision=HIGHEST)
    inverse = lower_inverse(jnp.linalg.cholesky(gram))
    basis = math.sqrt(total) * jnp.dot(inverse, flattened, precision=HIGHEST)
    tests = probes[1].astype(jnp.float32).reshape(NS, -1)
    coefficients = jnp.dot(basis, tests.T, precision=HIGHEST) / total
    projected = tests - jnp.dot(coefficients.T, basis, precision=HIGHEST)
    stacked = jnp.concatenate([basis, projected], axis=0).reshape((2 * NS,) + latent.shape)
    images = lax.map(single_image, stacked)
    basis_images = images[:NS]
    test_images = images[NS:]
    basis_forms = lax.optimization_barrier(jnp.sum(basis_images.reshape(NS, -1) * basis, axis=1))
    test_forms = lax.optimization_barrier(jnp.sum(test_images.reshape(NS, -1) * projected, axis=1))
    test_norms = lax.optimization_barrier(jnp.sum(projected * projected, axis=1))
    rayleigh = jnp.stack([basis_forms / total, test_forms / test_norms])
    divergence = (jnp.sum(basis_forms) / total + jnp.sum(test_forms) / NS) / total
    return (block_out, basis.reshape((NS,) + latent.shape), basis_images.astype(jnp.bfloat16), test_images.astype(jnp.bfloat16), rayleigh, divergence)
```

```python
import functools
import math

import jax
import jax.numpy as jnp
import numpy as np
from jax import lax
from jax.experimental import pallas as pl
from jax.experimental.pallas import tpu as pltpu
from jax.sharding import PartitionSpec as P

C = 320
GROUPS = 32
HEADS = 8
HEAD_DIM = 40
EPS = 1e-05
HIGHEST = lax.Precision.HIGHEST
F32 = jnp.float32
BF16 = jnp.bfloat16
CHUNK = HEADS


def dot(a, b):
    return jnp.dot(a, b, preferred_element_type=F32)


def hdot(a, b):
    return jnp.dot(a, b, preferred_element_type=F32, precision=HIGHEST)


def ndot(a, b, precision=None):
    return lax.dot_general(
        a, b, (((1,), (1,)), ((), ())), preferred_element_type=F32, precision=precision
    )


def iota(shape, dim):
    return lax.broadcasted_iota(jnp.int32, shape, dim)


def same_block(rows, columns, block):
    return (iota((rows, columns), 0) // block) == (iota((rows, columns), 1) // block)


def group_matrix():
    return (np.arange(C)[:, None] // (C // GROUPS) == np.arange(GROUPS)[None, :]).astype(np.float32)


def head_matrix():
    heads = np.arange(C) // HEAD_DIM
    return (heads[:, None] == heads[None, :]).astype(np.float32)


def head_rows():
    return (np.arange(HEADS)[:, None] == np.arange(C)[None, :] // HEAD_DIM).astype(np.float32)


def call(kernel, out_shape, *args, grid=None, in_specs=None, out_specs=None, flops=10**8):
    total = sum(a.size * a.dtype.itemsize for a in args)
    extra = {}
    if grid is not None:
        extra = dict(grid=grid, in_specs=in_specs, out_specs=out_specs)
    return pl.pallas_call(
        kernel,
        out_shape=out_shape,
        compiler_params=pltpu.CompilerParams(vmem_limit_bytes=56 * 2**20),
        cost_estimate=pl.CostEstimate(flops=flops, bytes_accessed=total, transcendentals=0),
        **extra,
    )(*args)


def sums_kernel(frames, with_latent, x_ref, t_ref, g_ref, out_ref):
    cols = x_ref.shape[0]
    count = t_ref.shape[1] // frames
    first = jnp.zeros((count, frames, C), F32)
    cross = jnp.zeros((count, frames, C), F32)
    lat = jnp.zeros((frames, C), F32)
    square = jnp.zeros((frames, C), F32)
    for w in range(cols):
        t = t_ref[w].astype(F32).reshape(count, frames, C)
        x = x_ref[w]
        first = first + t
        cross = cross + t * x[None]
        lat = lat + x
        square = square + x * x
    rows = [jnp.sum(first, axis=1), jnp.sum(cross, axis=1)]
    if with_latent:
        rows.append(jnp.broadcast_to(jnp.sum(lat, axis=0, keepdims=True), (8, C)))
        rows.append(jnp.broadcast_to(jnp.sum(square, axis=0, keepdims=True), (8, C)))
    out_ref[...] = hdot(jnp.concatenate(rows, axis=0), g_ref[...])


def latent_stats(ls_ref, members, gt):
    sums = ls_ref[...]
    mean = sums[0:1] / members
    inv = lax.rsqrt(sums[8:9] / members - mean * mean + EPS)
    return mean, inv


def conv_rows(act, w_ref, cols, per):
    total = None
    left = None
    right = None
    span = cols * per
    for a in range(3):
        mid = dot(act[a], w_ref[3 * a + 1])
        lo = dot(act[a][: span - per], w_ref[3 * a])
        hi = dot(act[a][per:], w_ref[3 * a + 2])
        total = mid if total is None else total + mid
        left = lo if left is None else left + lo
        right = hi if right is None else right + hi
    zero = jnp.zeros((per, C), F32)
    return (
        total + jnp.concatenate([zero, left], axis=0) + jnp.concatenate([right, zero], axis=0)
    )


def conv_frames(signal, w_ref, frames):
    rows = signal.shape[0]
    place = lax.rem(iota((rows, C), 0), frames)
    before = pltpu.roll(dot(signal, w_ref[0]), 1, 0)
    after = pltpu.roll(dot(signal, w_ref[2]), rows - 1, 0)
    return (
        dot(signal, w_ref[1])
        + jnp.where(place > 0, before, 0.0)
        + jnp.where(place < frames - 1, after, 0.0)
    )


def primal_kernel(
    members,
    edge_ref,
    temper_ref,
    lo_ref,
    x_ref,
    hi_ref,
    ls_ref,
    gain_ref,
    bias_ref,
    sb_ref,
    tb_ref,
    ws_ref,
    wt_ref,
    wqkv_ref,
    wo_ref,
    gt_ref,
    hh_ref,
    out_ref,
    a_ref,
    b_ref,
    qk_ref,
    kexp_ref,
    qexp_ref,
    vexp_ref,
    w_ref,
    wbd_ref,
):
    cols, frames = x_ref.shape[0], x_ref.shape[1]
    rows = cols * frames
    hf = HEADS * frames
    mean, inv = latent_stats(ls_ref, members, None)
    mean = hdot(mean + jnp.zeros((8, GROUPS), F32), gt_ref[...])[0:1]
    inv = hdot(inv + jnp.zeros((8, GROUPS), F32), gt_ref[...])[0:1]
    gain = gain_ref[...]
    acts = []
    for r, ref in enumerate((lo_ref, x_ref, hi_ref)):
        centered = ref[...].reshape(rows, C) - mean
        normed = centered * inv * gain + bias_ref[...]
        sig = jax.nn.sigmoid(normed)
        slope = sig * (1.0 + normed * (1.0 - sig)) * gain
        active = normed * sig
        if r != 1:
            keep = edge_ref[r // 2]
            slope = slope * keep
            active = active * keep
        a_ref[r] = (slope * inv).reshape(cols, frames, C)
        b_ref[r] = (slope * centered).reshape(cols, frames, C)
        acts.append(active.astype(BF16))
    spatial = (conv_rows(acts, ws_ref, cols, frames) + sb_ref[...]).astype(BF16)
    residual = x_ref[...].reshape(rows, C) + tb_ref[...] + conv_frames(spatial, wt_ref, frames)
    rounded = residual.astype(BF16)
    q = dot(rounded, wqkv_ref[0])
    k = dot(rounded, wqkv_ref[1])
    v = dot(rounded, wqkv_ref[2])
    hh = hh_ref[...]
    rq = 1.0 / jnp.sqrt(hdot(q * q, hh) / HEAD_DIM + 1.0)
    rk = 1.0 / jnp.sqrt(hdot(k * k, hh) / HEAD_DIM + 1.0)
    shape = (cols, frames, C)
    qk_ref[0] = q.reshape(shape)
    qk_ref[1] = (q * rq * rq * rq).reshape(shape)
    qk_ref[2] = rq.reshape(shape)
    qk_ref[3] = k.reshape(shape)
    qk_ref[4] = (k * rk * rk * rk).reshape(shape)
    qk_ref[5] = rk.reshape(shape)
    qu = q * rq
    ku = k * rk
    head_of_row = iota((hf, C), 0) // frames
    channel = iota((hf, C), 1)
    mask = jnp.where(
        (channel >= head_of_row * HEAD_DIM) & (channel < (head_of_row + 1) * HEAD_DIM), 1.0, 0.0
    )
    scale = jnp.zeros((hf, C), F32)
    for h in range(HEADS):
        scale = jnp.where(head_of_row == h, temper_ref[h] / math.sqrt(HEAD_DIM), scale)
    scale = scale * mask
    segment = jnp.where(same_block(hf, hf, frames), 1.0, 0.0)
    ei = iota((hf, HEADS * hf), 0)
    ej = iota((hf, HEADS * hf), 1)
    spread = jnp.where(
        (ei // frames == ej // hf) & (lax.rem(ei, frames) == lax.rem(ej, frames)), 1.0, 0.0
    ).astype(BF16)
    di = iota((hf, HEADS * hf), 0) // frames
    dj = lax.rem(ej, hf) // frames
    diagonal = jnp.where(di == dj, 1.0, 0.0)
    mixes = []
    for w in range(cols):
        part = slice(w * frames, (w + 1) * frames)
        k_rows = jnp.concatenate([ku[part]] * HEADS, axis=0) * scale
        q_rows = jnp.concatenate([qu[part]] * HEADS, axis=0) * scale
        v_rows = jnp.concatenate([v[part]] * HEADS, axis=0) * mask
        kexp_ref[w] = k_rows.astype(BF16)
        qexp_ref[w] = q_rows.astype(BF16)
        vexp_ref[w] = v_rows.astype(BF16)
        exponent = jnp.exp(ndot(qu[part], k_rows, HIGHEST))
        weights = exponent / hdot(exponent, segment)
        w_ref[w] = weights
        mixes.append(hdot(weights, v_rows))
        wide = dot(weights.astype(BF16), spread)
        wbd_ref[w] = (jnp.concatenate([wide] * CHUNK, axis=0) * diagonal).astype(BF16)
    mixture = jnp.concatenate(mixes, axis=0).astype(BF16)
    out_ref[...] = (residual + dot(mixture, wo_ref[...])).astype(BF16).reshape(shape)


def tangent_kernel(
    members,
    lo_ref,
    t_ref,
    hi_ref,
    first_ref,
    cross_ref,
    ls_ref,
    ws_ref,
    wt_ref,
    wqkv_ref,
    wo_ref,
    gt_ref,
    hh_ref,
    hrow_ref,
    a_ref,
    b_ref,
    qk_ref,
    kexp_ref,
    qexp_ref,
    vexp_ref,
    w_ref,
    wbd_ref,
    out_ref,
):
    cols, frames = a_ref.shape[1], a_ref.shape[2]
    per = CHUNK * frames
    hf = HEADS * frames
    mean, inv = latent_stats(ls_ref, members, None)
    first = first_ref[...]
    d_mean = first / members
    d_var = 2.0 * (cross_ref[...] - mean * first) / members
    d_std = -0.5 * inv * inv * inv * d_var
    d_mean = hdot(d_mean, gt_ref[...])[:, None, :]
    d_std = hdot(d_std, gt_ref[...])[:, None, :]
    acts = []
    for r, ref in enumerate((lo_ref, t_ref, hi_ref)):
        pieces = []
        for w in range(cols):
            t = ref[w].astype(F32).reshape(CHUNK, frames, C)
            piece = a_ref[r, w][None] * (t - d_mean) + b_ref[r, w][None] * d_std
            pieces.append(piece.reshape(per, C).astype(BF16))
        acts.append(jnp.concatenate(pieces, axis=0))
    spatial = conv_rows(acts, ws_ref, cols, per).astype(BF16)
    residual = t_ref[...].reshape(cols * per, C).astype(F32) + conv_frames(spatial, wt_ref, frames)
    rounded = residual.astype(BF16)
    shape = (cols, CHUNK, frames, C)
    hh = hh_ref[...].astype(BF16)

    def unit_shift(base, projection):
        value, cube, inverse = (qk_ref[base + i][:, None] for i in range(3))
        moved = dot(rounded, projection).reshape(shape)
        along = dot((value * moved).reshape(cols * per, C).astype(BF16), hh) * (1.0 / HEAD_DIM)
        return (moved * inverse - cube * along.reshape(shape)).reshape(cols * per, C).astype(BF16)

    dqu = unit_shift(0, wqkv_ref[0])
    dku = unit_shift(3, wqkv_ref[1])
    dv = dot(rounded, wqkv_ref[2])
    on_diagonal = same_block(hf, per, frames)
    segment = jnp.where(same_block(hf, hf, frames), 1.0, 0.0).astype(BF16)
    mixes = []
    for w in range(cols):
        part = slice(w * per, (w + 1) * per)
        scores = ndot(dqu[part], kexp_ref[w])
        turned = ndot(qexp_ref[w], dku[part])
        for d in range(HEADS):
            moved = pltpu.roll(turned, d * frames, 1) if d else turned
            moved = jnp.where(on_diagonal, moved, 0.0)
            if d:
                moved = jnp.concatenate([moved[d * frames :], moved[: d * frames]], axis=0)
            scores = scores + moved
        weights = jnp.concatenate([w_ref[w]] * CHUNK, axis=0)
        weighted = weights * scores
        top = weighted.astype(BF16)
        rest = (weighted - top.astype(F32)).astype(BF16)
        shift = weighted - weights * (dot(top, segment) + dot(rest, segment))
        own = dv[part]
        heads = [(own * hrow_ref[h : h + 1]).astype(BF16) for h in range(HEADS)]
        mix = dot(shift.astype(BF16), vexp_ref[w]) + dot(
            wbd_ref[w], jnp.concatenate(heads, axis=0)
        )
        mixes.append(mix.astype(BF16))
    result = residual + dot(jnp.concatenate(mixes, axis=0), wo_ref[...])
    out_ref[...] = result.reshape(cols, per, C).astype(out_ref.dtype)


def gather_rows(ref, w):
    return jnp.concatenate([ref[p, w] for p in range(ref.shape[0])], axis=0)


def gram_kernel(frames, s_ref, t_ref, out_ref):
    cols = t_ref.shape[0]
    total = None
    for w in range(cols):
        s = gather_rows(s_ref, w)
        term = ndot(jnp.concatenate([s, t_ref[w]], axis=0), s)
        total = term if total is None else total + term
    rows, columns = total.shape
    same = lax.rem(iota((rows, columns), 0), frames) == lax.rem(iota((rows, columns), 1), frames)
    total = jnp.where(same, total, 0.0)
    summed = jnp.sum(total.reshape(rows // frames, frames, columns), axis=1)
    fold = jnp.where(
        iota((columns, columns // frames), 0) // frames == iota((columns, columns // frames), 1),
        1.0,
        0.0,
    )
    out_ref[...] = hdot(summed, fold)


def combine_kernel(
    frames, total, slot_ref, gram_ref, s_ref, js_ref, t_ref, jt_ref, basis_ref, bi_ref, ti_ref, f_ref
):
    cols = t_ref.shape[0]
    ns = gram_ref.shape[1]
    own = gram_ref.shape[0] - ns
    gram = gram_ref[:ns, :]
    cross = gram_ref[ns:, :]
    inverse = jnp.where(iota((ns, ns), 0) == iota((ns, ns), 1), 1.0, 0.0)
    row = iota((ns, ns), 0)
    for j in range(ns):
        scale = 1.0 / jnp.sqrt(gram[j : j + 1, j : j + 1])
        column = gram[:, j : j + 1] * scale
        upper = gram[j : j + 1, :] * scale
        lower = inverse[j : j + 1, :] * scale
        gram = jnp.where(row > j, gram - column * upper, gram)
        inverse = jnp.where(row > j, inverse - column * lower, jnp.where(row == j, lower, inverse))
    first = slot_ref[0]
    pick = jnp.where(iota((own, ns), 1) == iota((own, ns), 0) + first, 1.0, 0.0)
    to_basis = math.sqrt(total) * hdot(pick, inverse)
    to_project = hdot(ndot(cross, inverse, HIGHEST), inverse)
    big, wide = own * frames, ns * frames
    spread_rows = jnp.where(iota((big, own), 0) // frames == iota((big, own), 1), 1.0, 0.0)
    spread_columns = jnp.where(iota((ns, wide), 1) // frames == iota((ns, wide), 0), 1.0, 0.0)
    same = lax.rem(iota((big, wide), 0), frames) == lax.rem(iota((big, wide), 1), frames)

    def expand(matrix):
        full = jnp.where(same, hdot(spread_rows, hdot(matrix, spread_columns)), 0.0)
        parts = []
        for _ in range(3):
            piece = full.astype(BF16)
            parts.append(piece)
            full = full - piece.astype(F32)
        return parts

    basis_parts = expand(to_basis)
    project_parts = expand(to_project)

    def apply(parts, array):
        result = dot(parts[0], array)
        for piece in parts[1:]:
            result = result + dot(piece, array)
        return result

    sums = [jnp.zeros((big, C), F32) for _ in range(3)]
    for w in range(cols):
        s = gather_rows(s_ref, w)
        js = gather_rows(js_ref, w)
        basis = apply(basis_parts, s)
        projected = t_ref[w].astype(F32) - apply(project_parts, s)
        basis_image = apply(basis_parts[:2], js)
        test_image = jt_ref[w] - apply(project_parts[:2], js)
        basis_ref[w] = basis
        bi_ref[w] = basis_image.astype(BF16)
        ti_ref[w] = test_image.astype(BF16)
        sums[0] = sums[0] + basis * basis_image
        sums[1] = sums[1] + projected * test_image
        sums[2] = sums[2] + projected * projected
    lane = iota((own, 128), 1)
    forms = jnp.zeros((own, 128), F32)
    for i in range(3):
        value = jnp.sum(jnp.sum(sums[i].reshape(own, frames, C), axis=1), axis=1, keepdims=True)
        forms = jnp.where(lane == i, value, forms)
    f_ref[...] = forms


def on_device(
    latent,
    probes,
    gn_gain,
    gn_bias,
    w_spatial,
    spatial_bias,
    w_temporal,
    temporal_bias,
    w_qkv,
    w_out,
    temper,
):
    frames, cols = latent.shape[0], latent.shape[2]
    own = probes.shape[1]
    tiles, shares = lax.axis_size("tile"), lax.axis_size("probe")
    ns = own * shares
    padded = -(-own // CHUNK) * CHUNK
    total = latent.size * tiles
    members = total // GROUPS
    hf = HEADS * frames
    here = lax.axis_index("tile")
    first_slot = lax.axis_index("probe") * own

    x = jnp.swapaxes(latent[:, 0], 0, 1)
    p = jnp.transpose(probes[:, :, :, 0], (3, 0, 1, 2, 4))
    if padded != own:
        p = jnp.pad(p, ((0, 0), (0, 0), (0, padded - own), (0, 0), (0, 0)))
    p = p.reshape(cols, 2 * padded * frames, C)
    forward = [(i, i + 1) for i in range(tiles - 1)]
    backward = [(j, i) for i, j in forward]

    def neighbours(block):
        return lax.ppermute(block, "tile", forward), lax.ppermute(block, "tile", backward)

    x_lo, x_hi = neighbours(x)
    p_lo, p_hi = neighbours(p)
    group = jnp.asarray(group_matrix())
    group_t = jnp.asarray(group_matrix().T)
    hh = jnp.asarray(head_matrix())
    hrow = jnp.asarray(head_rows())
    sums = call(
        functools.partial(sums_kernel, frames, True),
        jax.ShapeDtypeStruct((4 * padded + 16, GROUPS), F32),
        x,
        p,
        group,
    )
    sums = lax.psum(sums, "tile")
    latent_sums = sums[4 * padded :]
    wqkv = jnp.swapaxes(w_qkv, 0, 1)
    edge = jnp.stack([here > 0, here < tiles - 1]).astype(F32)

    smem = pl.BlockSpec(memory_space=pltpu.SMEM)
    vmem = pl.BlockSpec(memory_space=pltpu.VMEM)
    primal = pl.pallas_call(
        functools.partial(primal_kernel, members),
        in_specs=[smem, smem] + [vmem] * 14,
        out_shape=[
            jax.ShapeDtypeStruct((cols, frames, C), BF16),
            jax.ShapeDtypeStruct((3, cols, frames, C), F32),
            jax.ShapeDtypeStruct((3, cols, frames, C), F32),
            jax.ShapeDtypeStruct((6, cols, frames, C), F32),
            jax.ShapeDtypeStruct((cols, hf, C), BF16),
            jax.ShapeDtypeStruct((cols, hf, C), BF16),
            jax.ShapeDtypeStruct((cols, hf, C), BF16),
            jax.ShapeDtypeStruct((cols, frames, hf), F32),
            jax.ShapeDtypeStruct((cols, hf, HEADS * hf), BF16),
        ],
        compiler_params=pltpu.CompilerParams(vmem_limit_bytes=56 * 2**20),
        cost_estimate=pl.CostEstimate(flops=10**8, bytes_accessed=10**7, transcendentals=0),
    )(
        edge,
        temper,
        x_lo,
        x,
        x_hi,
        latent_sums,
        gn_gain[None],
        gn_bias[None],
        spatial_bias[None],
        temporal_bias[None],
        w_spatial,
        w_temporal,
        wqkv,
        w_out,
        group_t,
        hh,
    )
    block_out, caches = primal[0], primal[1:]
    chunks = padded // CHUNK
    per = CHUNK * frames

    def tangent(lo, mid, hi, offset, first, cross, dtype):
        fixed = (latent_sums, w_spatial, w_temporal, wqkv, w_out, group_t, hh, hrow) + tuple(caches)
        moving = pl.BlockSpec((cols, per, C), lambda i: (0, i + offset, 0))
        stat = pl.BlockSpec((CHUNK, GROUPS), lambda i: (i, 0))
        return call(
            functools.partial(tangent_kernel, members),
            jax.ShapeDtypeStruct((cols, padded * frames, C), dtype),
            lo,
            mid,
            hi,
            first,
            cross,
            *fixed,
            grid=(chunks,),
            in_specs=[moving] * 3 + [stat] * 2 + [vmem] * len(fixed),
            out_specs=pl.BlockSpec((cols, per, C), lambda i: (0, i, 0)),
            flops=2 * 10**9,
        )

    sketch = tangent(
        p_lo, p, p_hi, 0, sums[:padded], sums[2 * padded : 3 * padded], BF16
    )
    s_lo, s_hi = neighbours(sketch)
    s_sums = call(
        functools.partial(sums_kernel, frames, False),
        jax.ShapeDtypeStruct((2 * padded, GROUPS), F32),
        x,
        sketch,
        group,
    )
    s_sums = lax.psum(s_sums, "tile")
    s_all = lax.all_gather(sketch[:, : own * frames], "probe", axis=0)
    test = tangent(
        p_lo,
        p,
        p_hi,
        chunks,
        sums[padded : 2 * padded],
        sums[3 * padded : 4 * padded],
        F32,
    )
    p_test = p[:, padded * frames :]
    gram = call(
        functools.partial(gram_kernel, frames),
        jax.ShapeDtypeStruct((ns + padded, ns), F32),
        s_all,
        p_test,
    )
    gram = lax.psum(gram, "tile")
    second = tangent(s_lo, sketch, s_hi, 0, s_sums[:padded], s_sums[padded:], BF16)
    js_all = lax.all_gather(second[:, : own * frames], "probe", axis=0)
    image = (cols, padded * frames, C)
    basis, basis_images, test_images, forms = pl.pallas_call(
        functools.partial(combine_kernel, frames, total),
        in_specs=[smem] + [vmem] * 5,
        out_shape=[
            jax.ShapeDtypeStruct(image, F32),
            jax.ShapeDtypeStruct(image, BF16),
            jax.ShapeDtypeStruct(image, BF16),
            jax.ShapeDtypeStruct((padded, 128), F32),
        ],
        compiler_params=pltpu.CompilerParams(vmem_limit_bytes=56 * 2**20),
        cost_estimate=pl.CostEstimate(flops=10**9, bytes_accessed=10**7, transcendentals=0),
    )(first_slot.astype(jnp.int32)[None], gram, s_all, js_all, p_test, test)

    own_slots = first_slot + jnp.arange(own, dtype=jnp.int32)
    placed = jnp.arange(ns, dtype=jnp.int32)[None, :] == own_slots[:, None]
    placed = jnp.sum(jnp.where(placed[None], forms[:own, :3].T[:, :, None], 0.0), axis=1)
    placed = lax.psum(placed, ("tile", "probe"))
    rayleigh = jnp.stack([placed[0] / total, placed[1] / placed[2]])
    divergence = (jnp.sum(placed[0]) / total + jnp.sum(placed[1]) / ns) / total

    def restore(array):
        array = array.reshape(cols, padded, frames, C)[:, :own]
        return jnp.transpose(array, (1, 2, 0, 3))[:, :, None]

    return (
        jnp.swapaxes(block_out, 0, 1)[:, None],
        restore(basis),
        restore(basis_images),
        restore(test_images),
        rayleigh,
        divergence,
    )


def solution(mesh):
    in_specs = (
        P(None, "tile", None, None),
        P(None, "probe", None, "tile", None, None),
        P(),
        P(),
        P(),
        P(),
        P(),
        P(),
        P(),
        P(),
        P(),
    )
    out_specs = (
        P(None, "tile", None, None),
        P("probe", None, "tile", None, None),
        P("probe", None, "tile", None, None),
        P("probe", None, "tile", None, None),
        P(),
        P(),
    )
    return jax.shard_map(
        on_device, mesh=mesh, in_specs=in_specs, out_specs=out_specs, check_vma=False
    )
```

```python
import functools
import math

import jax
import jax.numpy as jnp
import numpy as np
from jax import lax
from jax.experimental import pallas as pl
from jax.experimental.pallas import tpu as pltpu
from jax.sharding import PartitionSpec as P

C = 320
GROUPS = 32
HEADS = 8
HEAD_DIM = 40
EPS = 1e-05
HIGHEST = lax.Precision.HIGHEST
F32 = jnp.float32
BF16 = jnp.bfloat16
CHUNK = HEADS


def dot(a, b):
    return jnp.dot(a, b, preferred_element_type=F32)


def hdot(a, b):
    return jnp.dot(a, b, preferred_element_type=F32, precision=HIGHEST)


def ndot(a, b, precision=None):
    return lax.dot_general(
        a, b, (((1,), (1,)), ((), ())), preferred_element_type=F32, precision=precision
    )


def iota(shape, dim):
    return lax.broadcasted_iota(jnp.int32, shape, dim)


def same_block(rows, columns, block):
    return (iota((rows, columns), 0) // block) == (iota((rows, columns), 1) // block)


def group_matrix():
    spread = np.zeros((4, C, 128), np.float32)
    for quarter in range(4):
        spread[quarter, np.arange(C), quarter * GROUPS + np.arange(C) // (C // GROUPS)] = 1.0
    return spread


def head_matrix():
    heads = np.arange(C) // HEAD_DIM
    return (heads[:, None] == heads[None, :]).astype(np.float32)


def head_rows():
    return (np.arange(HEADS)[:, None] == np.arange(C)[None, :] // HEAD_DIM).astype(np.float32)


def call(kernel, out_shape, *args, grid=None, in_specs=None, out_specs=None, flops=10**8):
    total = sum(a.size * a.dtype.itemsize for a in args)
    extra = {}
    if grid is not None:
        extra = dict(grid=grid, in_specs=in_specs, out_specs=out_specs)
    return pl.pallas_call(
        kernel,
        out_shape=out_shape,
        compiler_params=pltpu.CompilerParams(vmem_limit_bytes=56 * 2**20),
        cost_estimate=pl.CostEstimate(flops=flops, bytes_accessed=total, transcendentals=0),
        **extra,
    )(*args)


def image_sums(frames, sets, x_ref, t_ref, g_ref):
    cols = x_ref.shape[0]
    count = t_ref.shape[1] // frames
    first = jnp.zeros((count, frames, C), F32)
    cross = jnp.zeros((count, frames, C), F32)
    for w in range(cols):
        t = t_ref[w].astype(F32).reshape(count, frames, C)
        first = first + t
        cross = cross + t * x_ref[w][None]
    first = jnp.sum(first, axis=1)
    cross = jnp.sum(cross, axis=1)
    half = count // sets
    packed = jnp.zeros((half, 128), F32)
    for k in range(sets):
        part = slice(k * half, (k + 1) * half)
        packed = packed + hdot(first[part], g_ref[2 * k]) + hdot(cross[part], g_ref[2 * k + 1])
    return packed


def input_sums_kernel(frames, x_ref, t_ref, g_ref, out_ref):
    x = x_ref[...].reshape(-1, C)
    lat = jnp.broadcast_to(jnp.sum(x, axis=0, keepdims=True), (8, C))
    square = jnp.broadcast_to(jnp.sum(x * x, axis=0, keepdims=True), (8, C))
    out_ref[0:8] = hdot(lat, g_ref[0]) + hdot(square, g_ref[1])
    out_ref[8:] = image_sums(frames, 2, x_ref, t_ref, g_ref)


def reduce_kernel(axes, x_ref, out_ref, slots, send_sem, recv_sem):
    tiles, shares = lax.axis_size("tile"), lax.axis_size("probe")
    tile, share = lax.axis_index("tile"), lax.axis_index("probe")
    both = len(axes) == 2
    if both:
        count, me = tiles * shares, tile * shares + share
    elif axes[0] == "tile":
        count, me = tiles, tile
    else:
        count, me = shares, share

    def device(offset):
        other = lax.rem(me + offset, count)
        if both:
            return {"tile": other // shares, "probe": lax.rem(other, shares)}
        return {axes[0]: other}

    barrier = pltpu.get_barrier_semaphore()
    for offset in range(1, count):
        pl.semaphore_signal(
            barrier, inc=1, device_id=device(offset), device_id_type=pl.DeviceIdType.MESH
        )
    pl.semaphore_wait(barrier, count - 1)
    copies = []
    for offset in range(1, count):
        copy = pltpu.make_async_remote_copy(
            src_ref=x_ref,
            dst_ref=slots.at[me],
            send_sem=send_sem.at[offset - 1],
            recv_sem=recv_sem.at[offset - 1],
            device_id=device(offset),
            device_id_type=pl.DeviceIdType.MESH,
        )
        copy.start()
        copies.append(copy)
    slots[me] = x_ref[...]
    for copy in copies:
        copy.wait()
    total = slots[0]
    for i in range(1, count):
        total = total + slots[i]
    out_ref[...] = total


def reduce_over(array, axes, collective_id):
    count = math.prod(lax.axis_size(axis) for axis in axes)
    return pl.pallas_call(
        functools.partial(reduce_kernel, axes),
        out_shape=jax.ShapeDtypeStruct(array.shape, array.dtype),
        in_specs=[pl.BlockSpec(memory_space=pltpu.VMEM)],
        out_specs=pl.BlockSpec(memory_space=pltpu.VMEM),
        scratch_shapes=[
            pltpu.VMEM((count,) + array.shape, array.dtype),
            pltpu.SemaphoreType.DMA((count - 1,)),
            pltpu.SemaphoreType.DMA((count - 1,)),
        ],
        compiler_params=pltpu.CompilerParams(collective_id=collective_id, has_side_effects=True),
    )(array)


def latent_stats(ls_ref, members, gt_ref):
    sums = ls_ref[...]
    mean = hdot(sums, gt_ref[0])[0:1] / members
    inv = lax.rsqrt(hdot(sums, gt_ref[1])[0:1] / members - mean * mean + EPS)
    return mean, inv


def conv_rows(act, w_ref, cols, per):
    total = None
    left = None
    right = None
    span = cols * per
    for a in range(3):
        mid = dot(act[a], w_ref[3 * a + 1])
        lo = dot(act[a][: span - per], w_ref[3 * a])
        hi = dot(act[a][per:], w_ref[3 * a + 2])
        total = mid if total is None else total + mid
        left = lo if left is None else left + lo
        right = hi if right is None else right + hi
    zero = jnp.zeros((per, C), F32)
    return (
        total + jnp.concatenate([zero, left], axis=0) + jnp.concatenate([right, zero], axis=0)
    )


def conv_frames(signal, w_ref, frames):
    rows = signal.shape[0]
    place = lax.rem(iota((rows, C), 0), frames)
    before = pltpu.roll(dot(signal, w_ref[0]), 1, 0)
    after = pltpu.roll(dot(signal, w_ref[2]), rows - 1, 0)
    return (
        dot(signal, w_ref[1])
        + jnp.where(place > 0, before, 0.0)
        + jnp.where(place < frames - 1, after, 0.0)
    )


def primal_kernel(
    members,
    edge_ref,
    temper_ref,
    lo_ref,
    x_ref,
    hi_ref,
    ls_ref,
    gain_ref,
    bias_ref,
    sb_ref,
    tb_ref,
    ws_ref,
    wt_ref,
    wqkv_ref,
    wo_ref,
    gt_ref,
    hh_ref,
    out_ref,
    a_ref,
    b_ref,
    qk_ref,
    kexp_ref,
    qexp_ref,
    vexp_ref,
    w_ref,
    wbd_ref,
):
    cols, frames = x_ref.shape[0], x_ref.shape[1]
    rows = cols * frames
    hf = HEADS * frames
    mean, inv = latent_stats(ls_ref, members, gt_ref)
    gain = gain_ref[...]
    acts = []
    for r, ref in enumerate((lo_ref, x_ref, hi_ref)):
        centered = ref[...].reshape(rows, C) - mean
        normed = centered * inv * gain + bias_ref[...]
        sig = jax.nn.sigmoid(normed)
        slope = sig * (1.0 + normed * (1.0 - sig)) * gain
        active = normed * sig
        if r != 1:
            keep = edge_ref[r // 2]
            slope = slope * keep
            active = active * keep
        a_ref[r] = (slope * inv).reshape(cols, frames, C)
        b_ref[r] = (slope * centered).reshape(cols, frames, C)
        acts.append(active.astype(BF16))
    spatial = (conv_rows(acts, ws_ref, cols, frames) + sb_ref[...]).astype(BF16)
    residual = x_ref[...].reshape(rows, C) + tb_ref[...] + conv_frames(spatial, wt_ref, frames)
    rounded = residual.astype(BF16)
    q = dot(rounded, wqkv_ref[0])
    k = dot(rounded, wqkv_ref[1])
    v = dot(rounded, wqkv_ref[2])
    hh = hh_ref[...]
    rq = 1.0 / jnp.sqrt(hdot(q * q, hh) / HEAD_DIM + 1.0)
    rk = 1.0 / jnp.sqrt(hdot(k * k, hh) / HEAD_DIM + 1.0)
    shape = (cols, frames, C)
    qk_ref[0] = q.reshape(shape)
    qk_ref[1] = (q * rq * rq * rq).reshape(shape)
    qk_ref[2] = rq.reshape(shape)
    qk_ref[3] = k.reshape(shape)
    qk_ref[4] = (k * rk * rk * rk).reshape(shape)
    qk_ref[5] = rk.reshape(shape)
    qu = q * rq
    ku = k * rk
    head_of_row = iota((hf, C), 0) // frames
    channel = iota((hf, C), 1)
    mask = jnp.where(
        (channel >= head_of_row * HEAD_DIM) & (channel < (head_of_row + 1) * HEAD_DIM), 1.0, 0.0
    )
    scale = jnp.zeros((hf, C), F32)
    for h in range(HEADS):
        scale = jnp.where(head_of_row == h, temper_ref[h] / math.sqrt(HEAD_DIM), scale)
    scale = scale * mask
    segment = jnp.where(same_block(hf, hf, frames), 1.0, 0.0)
    ei = iota((hf, HEADS * hf), 0)
    ej = iota((hf, HEADS * hf), 1)
    spread = jnp.where(
        (ei // frames == ej // hf) & (lax.rem(ei, frames) == lax.rem(ej, frames)), 1.0, 0.0
    ).astype(BF16)
    di = iota((hf, HEADS * hf), 0) // frames
    dj = lax.rem(ej, hf) // frames
    diagonal = jnp.where(di == dj, 1.0, 0.0)
    mixes = []
    for w in range(cols):
        part = slice(w * frames, (w + 1) * frames)
        k_rows = jnp.concatenate([ku[part]] * HEADS, axis=0) * scale
        q_rows = jnp.concatenate([qu[part]] * HEADS, axis=0) * scale
        v_rows = jnp.concatenate([v[part]] * HEADS, axis=0) * mask
        kexp_ref[w] = k_rows.astype(BF16)
        qexp_ref[w] = q_rows.astype(BF16)
        vexp_ref[w] = v_rows.astype(BF16)
        exponent = jnp.exp(ndot(qu[part], k_rows, HIGHEST))
        weights = exponent / hdot(exponent, segment)
        w_ref[w] = weights
        mixes.append(hdot(weights, v_rows))
        wide = dot(weights.astype(BF16), spread)
        wbd_ref[w] = (jnp.concatenate([wide] * CHUNK, axis=0) * diagonal).astype(BF16)
    mixture = jnp.concatenate(mixes, axis=0).astype(BF16)
    out_ref[...] = (residual + dot(mixture, wo_ref[...])).astype(BF16).reshape(shape)


def tangent_kernel(
    members,
    which,
    lo_ref,
    t_ref,
    hi_ref,
    sums_ref,
    ls_ref,
    ws_ref,
    wt_ref,
    wqkv_ref,
    wo_ref,
    gt_ref,
    hh_ref,
    hrow_ref,
    a_ref,
    b_ref,
    qk_ref,
    kexp_ref,
    qexp_ref,
    vexp_ref,
    w_ref,
    wbd_ref,
    out_ref,
):
    cols, frames = a_ref.shape[1], a_ref.shape[2]
    per = CHUNK * frames
    hf = HEADS * frames
    mean, inv = latent_stats(ls_ref, members, gt_ref)
    first = hdot(sums_ref[...], gt_ref[2 * which])
    cross = hdot(sums_ref[...], gt_ref[2 * which + 1])
    d_mean = (first / members)[:, None, :]
    d_var = 2.0 * (cross - mean * first) / members
    d_std = (-0.5 * inv * inv * inv * d_var)[:, None, :]
    acts = []
    for r, ref in enumerate((lo_ref, t_ref, hi_ref)):
        pieces = []
        for w in range(cols):
            t = ref[w].astype(F32).reshape(CHUNK, frames, C)
            piece = a_ref[r, w][None] * (t - d_mean) + b_ref[r, w][None] * d_std
            pieces.append(piece.reshape(per, C).astype(BF16))
        acts.append(jnp.concatenate(pieces, axis=0))
    spatial = conv_rows(acts, ws_ref, cols, per).astype(BF16)
    residual = t_ref[...].reshape(cols * per, C).astype(F32) + conv_frames(spatial, wt_ref, frames)
    rounded = residual.astype(BF16)
    shape = (cols, CHUNK, frames, C)
    hh = hh_ref[...].astype(BF16)

    def unit_shift(base, projection):
        value, cube, inverse = (qk_ref[base + i][:, None] for i in range(3))
        moved = dot(rounded, projection).reshape(shape)
        along = dot((value * moved).reshape(cols * per, C).astype(BF16), hh) * (1.0 / HEAD_DIM)
        return (moved * inverse - cube * along.reshape(shape)).reshape(cols * per, C).astype(BF16)

    dqu = unit_shift(0, wqkv_ref[0])
    dku = unit_shift(3, wqkv_ref[1])
    dv = dot(rounded, wqkv_ref[2])
    on_diagonal = same_block(hf, per, frames)
    segment = jnp.where(same_block(hf, hf, frames), 1.0, 0.0).astype(BF16)
    mixes = []
    for w in range(cols):
        part = slice(w * per, (w + 1) * per)
        scores = ndot(dqu[part], kexp_ref[w])
        turned = ndot(qexp_ref[w], dku[part])
        for d in range(HEADS):
            moved = pltpu.roll(turned, d * frames, 1) if d else turned
            moved = jnp.where(on_diagonal, moved, 0.0)
            if d:
                moved = jnp.concatenate([moved[d * frames :], moved[: d * frames]], axis=0)
            scores = scores + moved
        weights = jnp.concatenate([w_ref[w]] * CHUNK, axis=0)
        weighted = weights * scores
        top = weighted.astype(BF16)
        rest = (weighted - top.astype(F32)).astype(BF16)
        shift = weighted - weights * (dot(top, segment) + dot(rest, segment))
        own = dv[part]
        heads = [(own * hrow_ref[h : h + 1]).astype(BF16) for h in range(HEADS)]
        mix = dot(shift.astype(BF16), vexp_ref[w]) + dot(
            wbd_ref[w], jnp.concatenate(heads, axis=0)
        )
        mixes.append(mix.astype(BF16))
    result = residual + dot(jnp.concatenate(mixes, axis=0), wo_ref[...])
    out_ref[...] = result.reshape(cols, per, C).astype(out_ref.dtype)


def gather_rows(ref, w, share):
    count = ref.shape[0]
    return jnp.concatenate(
        [ref[lax.rem(share - p + count, count), w] for p in range(count)], axis=0
    )


def gram_kernel(frames, slot_ref, x_ref, own_ref, s_ref, t_ref, g_ref, out_ref):
    cols = t_ref.shape[0]
    share = slot_ref[1]
    total = None
    for w in range(cols):
        s = gather_rows(s_ref, w, share)
        term = ndot(jnp.concatenate([s, t_ref[w]], axis=0), s)
        total = term if total is None else total + term
    rows, columns = total.shape
    same = lax.rem(iota((rows, columns), 0), frames) == lax.rem(iota((rows, columns), 1), frames)
    total = jnp.where(same, total, 0.0)
    summed = jnp.sum(total.reshape(rows // frames, frames, columns), axis=1)
    ns = columns // frames
    packed = image_sums(frames, 1, x_ref, own_ref, g_ref)
    own = packed.shape[0]
    for i in range(rows // frames // own):
        fold = jnp.where(
            iota((columns, 128), 0) // frames + (64 + i * ns) == iota((columns, 128), 1), 1.0, 0.0
        )
        packed = packed + hdot(summed[i * own : (i + 1) * own], fold)
    out_ref[...] = packed


def combine_kernel(
    frames, ns, total, slot_ref, gram_ref, s_ref, js_ref, t_ref, jt_ref, basis_ref, bi_ref, ti_ref, f_ref
):
    cols = t_ref.shape[0]
    own = gram_ref.shape[0]
    packed = gram_ref[...]
    pieces = []
    for i in range(ns // own + 1):
        choose = jnp.where(iota((128, ns), 0) == iota((128, ns), 1) + (64 + i * ns), 1.0, 0.0)
        pieces.append(hdot(packed, choose))
    gram = jnp.concatenate(pieces[:-1], axis=0)
    cross = pieces[-1]
    inverse = jnp.where(iota((ns, ns), 0) == iota((ns, ns), 1), 1.0, 0.0)
    row = iota((ns, ns), 0)
    for j in range(ns):
        scale = 1.0 / jnp.sqrt(gram[j : j + 1, j : j + 1])
        column = gram[:, j : j + 1] * scale
        upper = gram[j : j + 1, :] * scale
        lower = inverse[j : j + 1, :] * scale
        gram = jnp.where(row > j, gram - column * upper, gram)
        inverse = jnp.where(row > j, inverse - column * lower, jnp.where(row == j, lower, inverse))
    first = slot_ref[0]
    share = slot_ref[1]
    pick = jnp.where(iota((own, ns), 1) == iota((own, ns), 0) + first, 1.0, 0.0)
    to_basis = math.sqrt(total) * hdot(pick, inverse)
    to_project = hdot(ndot(cross, inverse, HIGHEST), inverse)
    big, wide = own * frames, ns * frames
    spread_rows = jnp.where(iota((big, own), 0) // frames == iota((big, own), 1), 1.0, 0.0)
    spread_columns = jnp.where(iota((ns, wide), 1) // frames == iota((ns, wide), 0), 1.0, 0.0)
    same = lax.rem(iota((big, wide), 0), frames) == lax.rem(iota((big, wide), 1), frames)

    def expand(matrix):
        full = jnp.where(same, hdot(spread_rows, hdot(matrix, spread_columns)), 0.0)
        parts = []
        for _ in range(3):
            piece = full.astype(BF16)
            parts.append(piece)
            full = full - piece.astype(F32)
        return parts

    basis_parts = expand(to_basis)
    project_parts = expand(to_project)

    def apply(parts, array):
        result = dot(parts[0], array)
        for piece in parts[1:]:
            result = result + dot(piece, array)
        return result

    sums = [jnp.zeros((big, C), F32) for _ in range(3)]
    for w in range(cols):
        s = gather_rows(s_ref, w, share)
        js = gather_rows(js_ref, w, share)
        basis = apply(basis_parts, s)
        projected = t_ref[w].astype(F32) - apply(project_parts, s)
        basis_image = apply(basis_parts[:2], js)
        test_image = jt_ref[w] - apply(project_parts[:2], js)
        basis_ref[w] = basis
        bi_ref[w] = basis_image.astype(BF16)
        ti_ref[w] = test_image.astype(BF16)
        sums[0] = sums[0] + basis * basis_image
        sums[1] = sums[1] + projected * test_image
        sums[2] = sums[2] + projected * projected
    lane = iota((own, 128), 1)
    forms = jnp.zeros((own, 128), F32)
    for i in range(3):
        value = jnp.sum(jnp.sum(sums[i].reshape(own, frames, C), axis=1), axis=1, keepdims=True)
        forms = jnp.where(lane == 4 * share + i, value, forms)
    f_ref[...] = forms


def on_device(
    latent,
    probes,
    gn_gain,
    gn_bias,
    w_spatial,
    spatial_bias,
    w_temporal,
    temporal_bias,
    w_qkv,
    w_out,
    temper,
):
    frames, cols = latent.shape[0], latent.shape[2]
    own = probes.shape[1]
    tiles, shares = lax.axis_size("tile"), lax.axis_size("probe")
    ns = own * shares
    padded = -(-own // CHUNK) * CHUNK
    total = latent.size * tiles
    members = total // GROUPS
    hf = HEADS * frames
    here = lax.axis_index("tile")
    first_slot = lax.axis_index("probe") * own

    x = jnp.swapaxes(latent[:, 0], 0, 1)
    p = jnp.transpose(probes[:, :, :, 0], (3, 0, 1, 2, 4))
    if padded != own:
        p = jnp.pad(p, ((0, 0), (0, 0), (0, padded - own), (0, 0), (0, 0)))
    p = p.reshape(cols, 2 * padded * frames, C)
    forward = [(i, i + 1) for i in range(tiles - 1)]
    backward = [(j, i) for i, j in forward]

    def neighbours(block):
        return lax.ppermute(block, "tile", forward), lax.ppermute(block, "tile", backward)

    x_lo, x_hi = neighbours(x)
    p_lo, p_hi = neighbours(p)
    group = jnp.asarray(group_matrix())
    group_t = jnp.asarray(np.swapaxes(group_matrix(), 1, 2))
    hh = jnp.asarray(head_matrix())
    hrow = jnp.asarray(head_rows())
    sums = call(
        functools.partial(input_sums_kernel, frames),
        jax.ShapeDtypeStruct((8 + padded, 128), F32),
        x,
        p,
        group,
    )
    sums = reduce_over(sums, ("tile",), 0)
    latent_sums, probe_sums = sums[:8], sums[8:]
    wqkv = jnp.swapaxes(w_qkv, 0, 1)
    edge = jnp.stack([here > 0, here < tiles - 1]).astype(F32)

    smem = pl.BlockSpec(memory_space=pltpu.SMEM)
    vmem = pl.BlockSpec(memory_space=pltpu.VMEM)
    primal = pl.pallas_call(
        functools.partial(primal_kernel, members),
        in_specs=[smem, smem] + [vmem] * 14,
        out_shape=[
            jax.ShapeDtypeStruct((cols, frames, C), BF16),
            jax.ShapeDtypeStruct((3, cols, frames, C), F32),
            jax.ShapeDtypeStruct((3, cols, frames, C), F32),
            jax.ShapeDtypeStruct((6, cols, frames, C), F32),
            jax.ShapeDtypeStruct((cols, hf, C), BF16),
            jax.ShapeDtypeStruct((cols, hf, C), BF16),
            jax.ShapeDtypeStruct((cols, hf, C), BF16),
            jax.ShapeDtypeStruct((cols, frames, hf), F32),
            jax.ShapeDtypeStruct((cols, hf, HEADS * hf), BF16),
        ],
        compiler_params=pltpu.CompilerParams(vmem_limit_bytes=56 * 2**20),
        cost_estimate=pl.CostEstimate(flops=10**8, bytes_accessed=10**7, transcendentals=0),
    )(
        edge,
        temper,
        x_lo,
        x,
        x_hi,
        latent_sums,
        gn_gain[None],
        gn_bias[None],
        spatial_bias[None],
        temporal_bias[None],
        w_spatial,
        w_temporal,
        wqkv,
        w_out,
        group_t,
        hh,
    )
    block_out, caches = primal[0], primal[1:]
    chunks = padded // CHUNK
    per = CHUNK * frames

    def tangent(lo, mid, hi, offset, sums, which, dtype):
        fixed = (latent_sums, w_spatial, w_temporal, wqkv, w_out, group_t, hh, hrow) + tuple(caches)
        moving = pl.BlockSpec((cols, per, C), lambda i: (0, i + offset, 0))
        stat = pl.BlockSpec((CHUNK, 128), lambda i: (i, 0))
        return call(
            functools.partial(tangent_kernel, members, which),
            jax.ShapeDtypeStruct((cols, padded * frames, C), dtype),
            lo,
            mid,
            hi,
            sums,
            *fixed,
            grid=(chunks,),
            in_specs=[moving] * 3 + [stat] + [vmem] * len(fixed),
            out_specs=pl.BlockSpec((cols, per, C), lambda i: (0, i, 0)),
            flops=2 * 10**9,
        )

    def from_shares(block):
        blocks = [block]
        for i in range(1, shares):
            ring = [(j, (j + i) % shares) for j in range(shares)]
            blocks.append(lax.ppermute(block, "probe", ring))
        return jnp.stack(blocks)

    slot = jnp.stack([first_slot, lax.axis_index("probe")]).astype(jnp.int32)
    sketch = tangent(p_lo, p, p_hi, 0, probe_sums, 0, BF16)
    s_lo, s_hi = neighbours(sketch)
    s_all = from_shares(sketch[:, : own * frames])
    test = tangent(p_lo, p, p_hi, chunks, probe_sums, 1, F32)
    p_test = p[:, padded * frames :]
    gram = pl.pallas_call(
        functools.partial(gram_kernel, frames),
        in_specs=[smem] + [vmem] * 5,
        out_shape=jax.ShapeDtypeStruct((padded, 128), F32),
        compiler_params=pltpu.CompilerParams(vmem_limit_bytes=56 * 2**20),
        cost_estimate=pl.CostEstimate(flops=10**9, bytes_accessed=10**7, transcendentals=0),
    )(slot, x, sketch, s_all, p_test, group)
    gram = reduce_over(gram, ("tile",), 1)
    second = tangent(s_lo, sketch, s_hi, 0, gram, 0, BF16)
    js_all = from_shares(second[:, : own * frames])
    image = (cols, padded * frames, C)
    basis, basis_images, test_images, forms = pl.pallas_call(
        functools.partial(combine_kernel, frames, ns, total),
        in_specs=[smem] + [vmem] * 5,
        out_shape=[
            jax.ShapeDtypeStruct(image, F32),
            jax.ShapeDtypeStruct(image, BF16),
            jax.ShapeDtypeStruct(image, BF16),
            jax.ShapeDtypeStruct((padded, 128), F32),
        ],
        compiler_params=pltpu.CompilerParams(vmem_limit_bytes=56 * 2**20),
        cost_estimate=pl.CostEstimate(flops=10**9, bytes_accessed=10**7, transcendentals=0),
    )(slot, gram, s_all, js_all, p_test, test)

    if tiles * shares <= 64:
        forms = reduce_over(forms, ("tile", "probe"), 2)
    else:
        forms = reduce_over(reduce_over(forms, ("tile",), 2), ("probe",), 3)
    placed = jnp.transpose(forms[:own, : 4 * shares].reshape(own, shares, 4), (2, 1, 0))
    placed = placed.reshape(4, ns)
    rayleigh = jnp.stack([placed[0] / total, placed[1] / placed[2]])
    divergence = (jnp.sum(placed[0]) / total + jnp.sum(placed[1]) / ns) / total

    def restore(array):
        array = array.reshape(cols, padded, frames, C)[:, :own]
        return jnp.transpose(array, (1, 2, 0, 3))[:, :, None]

    return (
        jnp.swapaxes(block_out, 0, 1)[:, None],
        restore(basis),
        restore(basis_images),
        restore(test_images),
        rayleigh,
        divergence,
    )


def solution(mesh):
    in_specs = (
        P(None, "tile", None, None),
        P(None, "probe", None, "tile", None, None),
        P(),
        P(),
        P(),
        P(),
        P(),
        P(),
        P(),
        P(),
        P(),
    )
    out_specs = (
        P(None, "tile", None, None),
        P("probe", None, "tile", None, None),
        P("probe", None, "tile", None, None),
        P("probe", None, "tile", None, None),
        P(),
        P(),
    )
    return jax.shard_map(
        on_device, mesh=mesh, in_specs=in_specs, out_specs=out_specs, check_vma=False
    )
```

```python
import functools
import math

import jax
import jax.numpy as jnp
import numpy as np
from jax import lax
from jax.experimental import pallas as pl
from jax.experimental.pallas import tpu as pltpu
from jax.sharding import PartitionSpec as P

C = 320
GROUPS = 32
HEADS = 8
HEAD_DIM = 40
EPS = 1e-05
HIGHEST = lax.Precision.HIGHEST
F32 = jnp.float32
BF16 = jnp.bfloat16
CHUNK = HEADS


def dot(a, b):
    return jnp.dot(a, b, preferred_element_type=F32)


def hdot(a, b):
    return jnp.dot(a, b, preferred_element_type=F32, precision=HIGHEST)


def ndot(a, b, precision=None):
    return lax.dot_general(
        a, b, (((1,), (1,)), ((), ())), preferred_element_type=F32, precision=precision
    )


def iota(shape, dim):
    return lax.broadcasted_iota(jnp.int32, shape, dim)


def same_block(rows, columns, block):
    return (iota((rows, columns), 0) // block) == (iota((rows, columns), 1) // block)


def group_matrix():
    spread = np.zeros((4, C, 128), np.float32)
    for quarter in range(4):
        spread[quarter, np.arange(C), quarter * GROUPS + np.arange(C) // (C // GROUPS)] = 1.0
    return spread


def head_matrix():
    heads = np.arange(C) // HEAD_DIM
    return (heads[:, None] == heads[None, :]).astype(np.float32)


def head_rows():
    return (np.arange(HEADS)[:, None] == np.arange(C)[None, :] // HEAD_DIM).astype(np.float32)


def call(kernel, out_shape, *args, grid=None, in_specs=None, out_specs=None, flops=10**8):
    total = sum(a.size * a.dtype.itemsize for a in args)
    extra = {}
    if grid is not None:
        extra = dict(grid=grid, in_specs=in_specs, out_specs=out_specs)
    return pl.pallas_call(
        kernel,
        out_shape=out_shape,
        compiler_params=pltpu.CompilerParams(vmem_limit_bytes=56 * 2**20),
        cost_estimate=pl.CostEstimate(flops=flops, bytes_accessed=total, transcendentals=0),
        **extra,
    )(*args)


def image_sums(frames, sets, x_ref, t_ref, g_ref):
    cols = x_ref.shape[0]
    count = t_ref.shape[1] // frames
    first = jnp.zeros((count, frames, C), F32)
    cross = jnp.zeros((count, frames, C), F32)
    for w in range(cols):
        t = t_ref[w].astype(F32).reshape(count, frames, C)
        first = first + t
        cross = cross + t * x_ref[w][None]
    first = jnp.sum(first, axis=1)
    cross = jnp.sum(cross, axis=1)
    half = count // sets
    packed = jnp.zeros((half, 128), F32)
    for k in range(sets):
        part = slice(k * half, (k + 1) * half)
        packed = packed + hdot(first[part], g_ref[2 * k]) + hdot(cross[part], g_ref[2 * k + 1])
    return packed


MESH = pl.DeviceIdType.MESH


class Halo:
    def __init__(self, tile, tiles, sources, lows, highs, send_sem, recv_sem):
        self.tile, self.tiles = tile, tiles
        self.up, self.down = [], []
        for i, (source, low, high) in enumerate(zip(sources, lows, highs)):
            for copies, target, place, slot in (
                (self.up, low, lax.rem(tile + 1, tiles), 2 * i),
                (self.down, high, lax.rem(tile + tiles - 1, tiles), 2 * i + 1),
            ):
                copies.append(
                    pltpu.make_async_remote_copy(
                        src_ref=source,
                        dst_ref=target,
                        send_sem=send_sem.at[slot],
                        recv_sem=recv_sem.at[slot],
                        device_id={"tile": place},
                        device_id_type=MESH,
                    )
                )

    def start(self):
        @pl.when(self.tile < self.tiles - 1)
        def _():
            for copy in self.up:
                copy.start()

        @pl.when(self.tile > 0)
        def _():
            for copy in self.down:
                copy.start()

    def wait(self):
        @pl.when(self.tile < self.tiles - 1)
        def _():
            for copy in self.up:
                copy.wait_send()
            for copy in self.down:
                copy.wait_recv()

        @pl.when(self.tile > 0)
        def _():
            for copy in self.down:
                copy.wait_send()
            for copy in self.up:
                copy.wait_recv()


def tile_sends(tile, tiles, source, slots, send_sem, recv_sem):
    return [
        pltpu.make_async_remote_copy(
            src_ref=source,
            dst_ref=slots.at[tile],
            send_sem=send_sem.at[offset - 1],
            recv_sem=recv_sem.at[offset - 1],
            device_id={"tile": lax.rem(tile + offset, tiles)},
            device_id_type=MESH,
        )
        for offset in range(1, tiles)
    ]


def signal_peers(axis, me, count):
    barrier = pltpu.get_barrier_semaphore()
    for offset in range(1, count):
        pl.semaphore_signal(
            barrier, inc=1, device_id={axis: lax.rem(me + offset, count)}, device_id_type=MESH
        )


def add_slots(slots):
    total = slots[0]
    for i in range(1, slots.shape[0]):
        total = total + slots[i]
    return total


def input_kernel(
    frames,
    x_ref,
    t_ref,
    g_ref,
    out_ref,
    x_lo,
    x_hi,
    t_lo,
    t_hi,
    mine,
    slots,
    send_sem,
    recv_sem,
    halo_send,
    halo_recv,
):
    tiles, tile = lax.axis_size("tile"), lax.axis_index("tile")
    signal_peers("tile", tile, tiles)
    x = x_ref[...].reshape(-1, C)
    lat = jnp.broadcast_to(jnp.sum(x, axis=0, keepdims=True), (8, C))
    square = jnp.broadcast_to(jnp.sum(x * x, axis=0, keepdims=True), (8, C))
    mine[0:8] = hdot(lat, g_ref[0]) + hdot(square, g_ref[1])
    mine[8:] = image_sums(frames, 2, x_ref, t_ref, g_ref)
    slots[tile] = mine[...]
    pl.semaphore_wait(pltpu.get_barrier_semaphore(), tiles - 1)
    halo = Halo(tile, tiles, (x_ref, t_ref), (x_lo, t_lo), (x_hi, t_hi), halo_send, halo_recv)
    sends = tile_sends(tile, tiles, mine, slots, send_sem, recv_sem)
    for copy in sends:
        copy.start()
    halo.start()
    for copy in sends:
        copy.wait()
    out_ref[...] = add_slots(slots)
    halo.wait()


def sketch_kernel(
    frames,
    own,
    x_ref,
    s_ref,
    t_ref,
    g_ref,
    out_ref,
    s_all,
    s_lo,
    s_hi,
    mine,
    slots,
    send_sem,
    recv_sem,
    halo_send,
    halo_recv,
    share_send,
    share_recv,
):
    tiles, tile = lax.axis_size("tile"), lax.axis_index("tile")
    shares, share = lax.axis_size("probe"), lax.axis_index("probe")
    signal_peers("tile", tile, tiles)
    signal_peers("probe", share, shares)
    s_all[0] = s_ref[:, : own * frames]
    pl.semaphore_wait(pltpu.get_barrier_semaphore(), tiles + shares - 2)
    source = s_ref if own * frames == s_ref.shape[1] else s_ref.at[:, : own * frames]
    gathers = [
        pltpu.make_async_remote_copy(
            src_ref=source,
            dst_ref=s_all.at[i],
            send_sem=share_send.at[i - 1],
            recv_sem=share_recv.at[i - 1],
            device_id={"probe": lax.rem(share + i, shares)},
            device_id_type=MESH,
        )
        for i in range(1, shares)
    ]
    for copy in gathers:
        copy.start()
    halo = Halo(tile, tiles, (s_ref,), (s_lo,), (s_hi,), halo_send, halo_recv)
    halo.start()
    packed = image_sums(frames, 1, x_ref, s_ref, g_ref)
    for copy in gathers:
        copy.wait()
    mine[...] = packed + pack_gram(frames, share, s_all, t_ref, packed.shape[0])
    slots[tile] = mine[...]
    sends = tile_sends(tile, tiles, mine, slots, send_sem, recv_sem)
    for copy in sends:
        copy.start()
    for copy in sends:
        copy.wait()
    out_ref[...] = add_slots(slots)
    halo.wait()


def reduce_kernel(axes, x_ref, out_ref, slots, send_sem, recv_sem):
    tiles, shares = lax.axis_size("tile"), lax.axis_size("probe")
    tile, share = lax.axis_index("tile"), lax.axis_index("probe")
    both = len(axes) == 2
    if both:
        count, me = tiles * shares, tile * shares + share
    elif axes[0] == "tile":
        count, me = tiles, tile
    else:
        count, me = shares, share

    def device(offset):
        other = lax.rem(me + offset, count)
        if both:
            return {"tile": other // shares, "probe": lax.rem(other, shares)}
        return {axes[0]: other}

    barrier = pltpu.get_barrier_semaphore()
    for offset in range(1, count):
        pl.semaphore_signal(
            barrier, inc=1, device_id=device(offset), device_id_type=pl.DeviceIdType.MESH
        )
    pl.semaphore_wait(barrier, count - 1)
    copies = []
    for offset in range(1, count):
        copy = pltpu.make_async_remote_copy(
            src_ref=x_ref,
            dst_ref=slots.at[me],
            send_sem=send_sem.at[offset - 1],
            recv_sem=recv_sem.at[offset - 1],
            device_id=device(offset),
            device_id_type=pl.DeviceIdType.MESH,
        )
        copy.start()
        copies.append(copy)
    slots[me] = x_ref[...]
    for copy in copies:
        copy.wait()
    total = slots[0]
    for i in range(1, count):
        total = total + slots[i]
    out_ref[...] = total


def reduce_over(array, axes, collective_id):
    count = math.prod(lax.axis_size(axis) for axis in axes)
    return pl.pallas_call(
        functools.partial(reduce_kernel, axes),
        out_shape=jax.ShapeDtypeStruct(array.shape, array.dtype),
        in_specs=[pl.BlockSpec(memory_space=pltpu.VMEM)],
        out_specs=pl.BlockSpec(memory_space=pltpu.VMEM),
        scratch_shapes=[
            pltpu.VMEM((count,) + array.shape, array.dtype),
            pltpu.SemaphoreType.DMA((count - 1,)),
            pltpu.SemaphoreType.DMA((count - 1,)),
        ],
        compiler_params=pltpu.CompilerParams(collective_id=collective_id, has_side_effects=True),
    )(array)


def latent_stats(ls_ref, members, gt_ref):
    sums = ls_ref[...]
    mean = hdot(sums, gt_ref[0])[0:1] / members
    inv = lax.rsqrt(hdot(sums, gt_ref[1])[0:1] / members - mean * mean + EPS)
    return mean, inv


def inside(r):
    tile = lax.axis_index("tile")
    return tile > 0 if r == 0 else tile < lax.axis_size("tile") - 1


def conv_rows(act, w_ref, cols, per):
    total = None
    left = None
    right = None
    span = cols * per
    for a in range(3):
        mid = dot(act[a], w_ref[3 * a + 1])
        lo = dot(act[a][: span - per], w_ref[3 * a])
        hi = dot(act[a][per:], w_ref[3 * a + 2])
        total = mid if total is None else total + mid
        left = lo if left is None else left + lo
        right = hi if right is None else right + hi
    zero = jnp.zeros((per, C), F32)
    return (
        total + jnp.concatenate([zero, left], axis=0) + jnp.concatenate([right, zero], axis=0)
    )


def conv_frames(signal, w_ref, frames):
    rows = signal.shape[0]
    place = lax.rem(iota((rows, C), 0), frames)
    before = pltpu.roll(dot(signal, w_ref[0]), 1, 0)
    after = pltpu.roll(dot(signal, w_ref[2]), rows - 1, 0)
    return (
        dot(signal, w_ref[1])
        + jnp.where(place > 0, before, 0.0)
        + jnp.where(place < frames - 1, after, 0.0)
    )


def primal_kernel(
    members,
    temper_ref,
    lo_ref,
    x_ref,
    hi_ref,
    ls_ref,
    vec_ref,
    ws_ref,
    wt_ref,
    wqkv_ref,
    wo_ref,
    gt_ref,
    hh_ref,
    out_ref,
    a_ref,
    b_ref,
    qk_ref,
    kexp_ref,
    qexp_ref,
    vexp_ref,
    w_ref,
    wbd_ref,
):
    cols, frames = x_ref.shape[0], x_ref.shape[1]
    rows = cols * frames
    hf = HEADS * frames
    mean, inv = latent_stats(ls_ref, members, gt_ref)
    gain = vec_ref[0:1]
    acts = []
    for r, ref in enumerate((lo_ref, x_ref, hi_ref)):
        value = ref[...].reshape(rows, C)
        if r != 1:
            value = jnp.where(inside(r), value, 0.0)
        centered = value - mean
        normed = centered * inv * gain + vec_ref[1:2]
        sig = jax.nn.sigmoid(normed)
        slope = sig * (1.0 + normed * (1.0 - sig)) * gain
        active = normed * sig
        if r != 1:
            keep = jnp.where(inside(r), 1.0, 0.0)
            slope = slope * keep
            active = active * keep
        a_ref[r] = (slope * inv).reshape(cols, frames, C)
        b_ref[r] = (slope * centered).reshape(cols, frames, C)
        acts.append(active.astype(BF16))
    spatial = (conv_rows(acts, ws_ref, cols, frames) + vec_ref[2:3]).astype(BF16)
    residual = x_ref[...].reshape(rows, C) + vec_ref[3:4] + conv_frames(spatial, wt_ref, frames)
    rounded = residual.astype(BF16)
    q = dot(rounded, wqkv_ref[0])
    k = dot(rounded, wqkv_ref[1])
    v = dot(rounded, wqkv_ref[2])
    hh = hh_ref[...]
    rq = 1.0 / jnp.sqrt(hdot(q * q, hh) / HEAD_DIM + 1.0)
    rk = 1.0 / jnp.sqrt(hdot(k * k, hh) / HEAD_DIM + 1.0)
    shape = (cols, frames, C)
    qk_ref[0] = q.reshape(shape)
    qk_ref[1] = (q * rq * rq * rq).reshape(shape)
    qk_ref[2] = rq.reshape(shape)
    qk_ref[3] = k.reshape(shape)
    qk_ref[4] = (k * rk * rk * rk).reshape(shape)
    qk_ref[5] = rk.reshape(shape)
    qu = q * rq
    ku = k * rk
    head_of_row = iota((hf, C), 0) // frames
    channel = iota((hf, C), 1)
    mask = jnp.where(
        (channel >= head_of_row * HEAD_DIM) & (channel < (head_of_row + 1) * HEAD_DIM), 1.0, 0.0
    )
    scale = jnp.zeros((hf, C), F32)
    for h in range(HEADS):
        scale = jnp.where(head_of_row == h, temper_ref[h] / math.sqrt(HEAD_DIM), scale)
    scale = scale * mask
    segment = jnp.where(same_block(hf, hf, frames), 1.0, 0.0)
    ei = iota((hf, HEADS * hf), 0)
    ej = iota((hf, HEADS * hf), 1)
    spread = jnp.where(
        (ei // frames == ej // hf) & (lax.rem(ei, frames) == lax.rem(ej, frames)), 1.0, 0.0
    ).astype(BF16)
    di = iota((hf, HEADS * hf), 0) // frames
    dj = lax.rem(ej, hf) // frames
    diagonal = jnp.where(di == dj, 1.0, 0.0)
    mixes = []
    for w in range(cols):
        part = slice(w * frames, (w + 1) * frames)
        k_rows = jnp.concatenate([ku[part]] * HEADS, axis=0) * scale
        q_rows = jnp.concatenate([qu[part]] * HEADS, axis=0) * scale
        v_rows = jnp.concatenate([v[part]] * HEADS, axis=0) * mask
        kexp_ref[w] = k_rows.astype(BF16)
        qexp_ref[w] = q_rows.astype(BF16)
        vexp_ref[w] = v_rows.astype(BF16)
        exponent = jnp.exp(ndot(qu[part], k_rows, HIGHEST))
        weights = exponent / hdot(exponent, segment)
        w_ref[w] = weights
        mixes.append(hdot(weights, v_rows))
        wide = dot(weights.astype(BF16), spread)
        wbd_ref[w] = (jnp.concatenate([wide] * CHUNK, axis=0) * diagonal).astype(BF16)
    mixture = jnp.concatenate(mixes, axis=0).astype(BF16)
    out_ref[...] = (residual + dot(mixture, wo_ref[...])).astype(BF16).reshape(shape)


def tangent_kernel(
    members,
    which,
    lo_ref,
    t_ref,
    hi_ref,
    sums_ref,
    ls_ref,
    ws_ref,
    wt_ref,
    wqkv_ref,
    wo_ref,
    gt_ref,
    hh_ref,
    hrow_ref,
    a_ref,
    b_ref,
    qk_ref,
    kexp_ref,
    qexp_ref,
    vexp_ref,
    w_ref,
    wbd_ref,
    out_ref,
):
    cols, frames = a_ref.shape[1], a_ref.shape[2]
    per = CHUNK * frames
    hf = HEADS * frames
    mean, inv = latent_stats(ls_ref, members, gt_ref)
    first = hdot(sums_ref[...], gt_ref[2 * which])
    cross = hdot(sums_ref[...], gt_ref[2 * which + 1])
    d_mean = (first / members)[:, None, :]
    d_var = 2.0 * (cross - mean * first) / members
    d_std = (-0.5 * inv * inv * inv * d_var)[:, None, :]
    acts = []
    for r, ref in enumerate((lo_ref, t_ref, hi_ref)):
        pieces = []
        for w in range(cols):
            t = ref[w].astype(F32).reshape(CHUNK, frames, C)
            if r != 1:
                t = jnp.where(inside(r), t, 0.0)
            piece = a_ref[r, w][None] * (t - d_mean) + b_ref[r, w][None] * d_std
            pieces.append(piece.reshape(per, C).astype(BF16))
        acts.append(jnp.concatenate(pieces, axis=0))
    spatial = conv_rows(acts, ws_ref, cols, per).astype(BF16)
    residual = t_ref[...].reshape(cols * per, C).astype(F32) + conv_frames(spatial, wt_ref, frames)
    rounded = residual.astype(BF16)
    shape = (cols, CHUNK, frames, C)
    hh = hh_ref[...].astype(BF16)

    def unit_shift(base, projection):
        value, cube, inverse = (qk_ref[base + i][:, None] for i in range(3))
        moved = dot(rounded, projection).reshape(shape)
        along = dot((value * moved).reshape(cols * per, C).astype(BF16), hh) * (1.0 / HEAD_DIM)
        return (moved * inverse - cube * along.reshape(shape)).reshape(cols * per, C).astype(BF16)

    dqu = unit_shift(0, wqkv_ref[0])
    dku = unit_shift(3, wqkv_ref[1])
    dv = dot(rounded, wqkv_ref[2])
    on_diagonal = same_block(hf, per, frames)
    segment = jnp.where(same_block(hf, hf, frames), 1.0, 0.0).astype(BF16)
    mixes = []
    for w in range(cols):
        part = slice(w * per, (w + 1) * per)
        scores = ndot(dqu[part], kexp_ref[w])
        turned = ndot(qexp_ref[w], dku[part])
        for d in range(HEADS):
            moved = pltpu.roll(turned, d * frames, 1) if d else turned
            moved = jnp.where(on_diagonal, moved, 0.0)
            if d:
                moved = jnp.concatenate([moved[d * frames :], moved[: d * frames]], axis=0)
            scores = scores + moved
        weights = jnp.concatenate([w_ref[w]] * CHUNK, axis=0)
        weighted = weights * scores
        top = weighted.astype(BF16)
        rest = (weighted - top.astype(F32)).astype(BF16)
        shift = weighted - weights * (dot(top, segment) + dot(rest, segment))
        own = dv[part]
        heads = [(own * hrow_ref[h : h + 1]).astype(BF16) for h in range(HEADS)]
        mix = dot(shift.astype(BF16), vexp_ref[w]) + dot(
            wbd_ref[w], jnp.concatenate(heads, axis=0)
        )
        mixes.append(mix.astype(BF16))
    result = residual + dot(jnp.concatenate(mixes, axis=0), wo_ref[...])
    out_ref[...] = result.reshape(cols, per, C).astype(out_ref.dtype)


def gather_rows(ref, w, share):
    count = ref.shape[0]
    return jnp.concatenate(
        [ref[lax.rem(share - p + count, count), w] for p in range(count)], axis=0
    )


def pack_gram(frames, share, s_ref, t_ref, own):
    cols = t_ref.shape[0]
    half = t_ref.shape[1] // 2
    total = None
    for w in range(cols):
        s = gather_rows(s_ref, w, share)
        term = ndot(jnp.concatenate([s, t_ref[w, half:]], axis=0), s)
        total = term if total is None else total + term
    rows, columns = total.shape
    same = lax.rem(iota((rows, columns), 0), frames) == lax.rem(iota((rows, columns), 1), frames)
    total = jnp.where(same, total, 0.0)
    summed = jnp.sum(total.reshape(rows // frames, frames, columns), axis=1)
    ns = columns // frames
    packed = jnp.zeros((own, 128), F32)
    for i in range(rows // frames // own):
        fold = jnp.where(
            iota((columns, 128), 0) // frames + (64 + i * ns) == iota((columns, 128), 1), 1.0, 0.0
        )
        packed = packed + hdot(summed[i * own : (i + 1) * own], fold)
    return packed


def combine_kernel(
    frames, ns, count, total, gram_ref, s_ref, js_ref, t_ref, jt_ref, basis_ref, bi_ref, ti_ref, f_ref
):
    cols = t_ref.shape[0]
    own = gram_ref.shape[0]
    packed = gram_ref[...]
    pieces = []
    for i in range(ns // own + 1):
        choose = jnp.where(iota((128, ns), 0) == iota((128, ns), 1) + (64 + i * ns), 1.0, 0.0)
        pieces.append(hdot(packed, choose))
    gram = jnp.concatenate(pieces[:-1], axis=0)
    cross = pieces[-1]
    inverse = jnp.where(iota((ns, ns), 0) == iota((ns, ns), 1), 1.0, 0.0)
    row = iota((ns, ns), 0)
    for j in range(ns):
        scale = 1.0 / jnp.sqrt(gram[j : j + 1, j : j + 1])
        column = gram[:, j : j + 1] * scale
        upper = gram[j : j + 1, :] * scale
        lower = inverse[j : j + 1, :] * scale
        gram = jnp.where(row > j, gram - column * upper, gram)
        inverse = jnp.where(row > j, inverse - column * lower, jnp.where(row == j, lower, inverse))
    share = lax.axis_index("probe")
    first = share * count
    pick = jnp.where(iota((own, ns), 1) == iota((own, ns), 0) + first, 1.0, 0.0)
    to_basis = math.sqrt(total) * hdot(pick, inverse)
    to_project = hdot(ndot(cross, inverse, HIGHEST), inverse)
    big, wide = own * frames, ns * frames
    spread_rows = jnp.where(iota((big, own), 0) // frames == iota((big, own), 1), 1.0, 0.0)
    spread_columns = jnp.where(iota((ns, wide), 1) // frames == iota((ns, wide), 0), 1.0, 0.0)
    same = lax.rem(iota((big, wide), 0), frames) == lax.rem(iota((big, wide), 1), frames)

    def expand(matrix):
        full = jnp.where(same, hdot(spread_rows, hdot(matrix, spread_columns)), 0.0)
        parts = []
        for _ in range(3):
            piece = full.astype(BF16)
            parts.append(piece)
            full = full - piece.astype(F32)
        return parts

    basis_parts = expand(to_basis)
    project_parts = expand(to_project)

    def apply(parts, array):
        result = dot(parts[0], array)
        for piece in parts[1:]:
            result = result + dot(piece, array)
        return result

    sums = [jnp.zeros((big, C), F32) for _ in range(3)]
    for w in range(cols):
        s = gather_rows(s_ref, w, share)
        js = gather_rows(js_ref, w, share)
        basis = apply(basis_parts, s)
        projected = t_ref[w, t_ref.shape[1] // 2 :].astype(F32) - apply(project_parts, s)
        basis_image = apply(basis_parts[:2], js)
        test_image = jt_ref[w] - apply(project_parts[:2], js)
        basis_ref[w] = basis
        bi_ref[w] = basis_image.astype(BF16)
        ti_ref[w] = test_image.astype(BF16)
        sums[0] = sums[0] + basis * basis_image
        sums[1] = sums[1] + projected * test_image
        sums[2] = sums[2] + projected * projected
    lane = iota((own, 128), 1)
    forms = jnp.zeros((own, 128), F32)
    for i in range(3):
        value = jnp.sum(jnp.sum(sums[i].reshape(own, frames, C), axis=1), axis=1, keepdims=True)
        forms = jnp.where(lane == 4 * share + i, value, forms)
    f_ref[...] = forms


def on_device(
    latent,
    probes,
    gn_gain,
    gn_bias,
    w_spatial,
    spatial_bias,
    w_temporal,
    temporal_bias,
    w_qkv,
    w_out,
    temper,
):
    frames, cols = latent.shape[0], latent.shape[2]
    own = probes.shape[1]
    tiles, shares = lax.axis_size("tile"), lax.axis_size("probe")
    ns = own * shares
    padded = -(-own // CHUNK) * CHUNK
    total = latent.size * tiles
    members = total // GROUPS
    hf = HEADS * frames

    x = jnp.swapaxes(latent[:, 0], 0, 1)
    p = jnp.transpose(probes[:, :, :, 0], (3, 0, 1, 2, 4))
    if padded != own:
        p = jnp.pad(p, ((0, 0), (0, 0), (0, padded - own), (0, 0), (0, 0)))
    p = p.reshape(cols, 2 * padded * frames, C)
    group = jnp.asarray(group_matrix())
    group_t = jnp.asarray(np.swapaxes(group_matrix(), 1, 2))
    hh = jnp.asarray(head_matrix())
    hrow = jnp.asarray(head_rows())
    smem = pl.BlockSpec(memory_space=pltpu.SMEM)
    vmem = pl.BlockSpec(memory_space=pltpu.VMEM)
    anywhere = pl.BlockSpec(memory_space=pl.ANY)

    def like(array):
        return jax.ShapeDtypeStruct(array.shape, array.dtype)

    def exchange(kernel, args, outs, out_specs, rows, halos, collective_id, extra=()):
        block = (rows, 128)
        semaphores = pltpu.SemaphoreType.DMA
        return pl.pallas_call(
            kernel,
            in_specs=[vmem] * len(args),
            out_shape=[jax.ShapeDtypeStruct(block, F32)] + outs,
            out_specs=[vmem] + out_specs,
            scratch_shapes=[
                pltpu.VMEM(block, F32),
                pltpu.VMEM((tiles,) + block, F32),
                semaphores((tiles - 1,)),
                semaphores((tiles - 1,)),
                semaphores((2 * halos,)),
                semaphores((2 * halos,)),
            ]
            + [semaphores(shape) for shape in extra],
            compiler_params=pltpu.CompilerParams(
                collective_id=collective_id,
                has_side_effects=True,
                vmem_limit_bytes=40 * 2**20,
            ),
        )(*args)

    sums, x_lo, x_hi, p_lo, p_hi = exchange(
        functools.partial(input_kernel, frames),
        (x, p, group),
        [like(x), like(x), like(p), like(p)],
        [anywhere] * 4,
        8 + padded,
        2,
        0,
    )
    latent_sums, probe_sums = sums[:8], sums[8:]
    wqkv = jnp.swapaxes(w_qkv, 0, 1)
    primal = pl.pallas_call(
        functools.partial(primal_kernel, members),
        in_specs=[smem] + [vmem] * 11,
        out_shape=[
            jax.ShapeDtypeStruct((cols, frames, C), BF16),
            jax.ShapeDtypeStruct((3, cols, frames, C), F32),
            jax.ShapeDtypeStruct((3, cols, frames, C), F32),
            jax.ShapeDtypeStruct((6, cols, frames, C), F32),
            jax.ShapeDtypeStruct((cols, hf, C), BF16),
            jax.ShapeDtypeStruct((cols, hf, C), BF16),
            jax.ShapeDtypeStruct((cols, hf, C), BF16),
            jax.ShapeDtypeStruct((cols, frames, hf), F32),
            jax.ShapeDtypeStruct((cols, hf, HEADS * hf), BF16),
        ],
        compiler_params=pltpu.CompilerParams(vmem_limit_bytes=56 * 2**20),
        cost_estimate=pl.CostEstimate(flops=10**8, bytes_accessed=10**7, transcendentals=0),
    )(
        temper,
        x_lo,
        x,
        x_hi,
        latent_sums,
        jnp.stack([gn_gain, gn_bias, spatial_bias, temporal_bias]),
        w_spatial,
        w_temporal,
        wqkv,
        w_out,
        group_t,
        hh,
    )
    block_out, caches = primal[0], primal[1:]
    chunks = padded // CHUNK
    per = CHUNK * frames

    def tangent(lo, mid, hi, offset, sums, which, dtype):
        fixed = (latent_sums, w_spatial, w_temporal, wqkv, w_out, group_t, hh, hrow) + tuple(caches)
        moving = pl.BlockSpec((cols, per, C), lambda i: (0, i + offset, 0))
        stat = pl.BlockSpec((CHUNK, 128), lambda i: (i, 0))
        return call(
            functools.partial(tangent_kernel, members, which),
            jax.ShapeDtypeStruct((cols, padded * frames, C), dtype),
            lo,
            mid,
            hi,
            sums,
            *fixed,
            grid=(chunks,),
            in_specs=[moving] * 3 + [stat] + [vmem] * len(fixed),
            out_specs=pl.BlockSpec((cols, per, C), lambda i: (0, i, 0)),
            flops=2 * 10**9,
        )

    def from_shares(block):
        blocks = [block]
        for i in range(1, shares):
            ring = [(j, (j + i) % shares) for j in range(shares)]
            blocks.append(lax.ppermute(block, "probe", ring))
        return jnp.stack(blocks)

    sketch = tangent(p_lo, p, p_hi, 0, probe_sums, 0, BF16)
    gram, s_all, s_lo, s_hi = exchange(
        functools.partial(sketch_kernel, frames, own),
        (x, sketch, p, group),
        [jax.ShapeDtypeStruct((shares, cols, own * frames, C), BF16), like(sketch), like(sketch)],
        [vmem, anywhere, anywhere],
        padded,
        1,
        1,
        [(shares - 1,), (shares - 1,)],
    )
    test = tangent(p_lo, p, p_hi, chunks, probe_sums, 1, F32)
    second = tangent(s_lo, sketch, s_hi, 0, gram, 0, BF16)
    js_all = from_shares(second[:, : own * frames])
    image = (cols, padded * frames, C)
    basis, basis_images, test_images, forms = pl.pallas_call(
        functools.partial(combine_kernel, frames, ns, own, total),
        in_specs=[vmem] * 5,
        out_shape=[
            jax.ShapeDtypeStruct(image, F32),
            jax.ShapeDtypeStruct(image, BF16),
            jax.ShapeDtypeStruct(image, BF16),
            jax.ShapeDtypeStruct((padded, 128), F32),
        ],
        compiler_params=pltpu.CompilerParams(vmem_limit_bytes=56 * 2**20),
        cost_estimate=pl.CostEstimate(flops=10**9, bytes_accessed=10**7, transcendentals=0),
    )(gram, s_all, js_all, p, test)

    if tiles * shares <= 64:
        forms = reduce_over(forms, ("tile", "probe"), 2)
    else:
        forms = reduce_over(reduce_over(forms, ("tile",), 2), ("probe",), 3)
    placed = jnp.transpose(forms[:own, : 4 * shares].reshape(own, shares, 4), (2, 1, 0))
    placed = placed.reshape(4, ns)
    rayleigh = jnp.stack([placed[0] / total, placed[1] / placed[2]])
    divergence = (jnp.sum(placed[0]) / total + jnp.sum(placed[1]) / ns) / total

    def restore(array):
        array = array.reshape(cols, padded, frames, C)[:, :own]
        return jnp.transpose(array, (1, 2, 0, 3))[:, :, None]

    return (
        jnp.swapaxes(block_out, 0, 1)[:, None],
        restore(basis),
        restore(basis_images),
        restore(test_images),
        rayleigh,
        divergence,
    )


def solution(mesh):
    in_specs = (
        P(None, "tile", None, None),
        P(None, "probe", None, "tile", None, None),
        P(),
        P(),
        P(),
        P(),
        P(),
        P(),
        P(),
        P(),
        P(),
    )
    out_specs = (
        P(None, "tile", None, None),
        P("probe", None, "tile", None, None),
        P("probe", None, "tile", None, None),
        P("probe", None, "tile", None, None),
        P(),
        P(),
    )
    return jax.shard_map(
        on_device, mesh=mesh, in_specs=in_specs, out_specs=out_specs, check_vma=False
    )
```

```python
import functools
import math

import jax
import jax.numpy as jnp
import numpy as np
from jax import lax
from jax.experimental import pallas as pl
from jax.experimental.pallas import tpu as pltpu
from jax.sharding import PartitionSpec as P

C = 320
GROUPS = 32
HEADS = 8
HEAD_DIM = 40
EPS = 1e-05
HIGHEST = lax.Precision.HIGHEST
F32 = jnp.float32
BF16 = jnp.bfloat16
CHUNK = HEADS


def dot(a, b):
    return jnp.dot(a, b, preferred_element_type=F32)


def hdot(a, b):
    return jnp.dot(a, b, preferred_element_type=F32, precision=HIGHEST)


def ndot(a, b, precision=None):
    return lax.dot_general(
        a, b, (((1,), (1,)), ((), ())), preferred_element_type=F32, precision=precision
    )


def iota(shape, dim):
    return lax.broadcasted_iota(jnp.int32, shape, dim)


def same_block(rows, columns, block):
    return (iota((rows, columns), 0) // block) == (iota((rows, columns), 1) // block)


def group_matrix():
    spread = np.zeros((4, C, 128), np.float32)
    for quarter in range(4):
        spread[quarter, np.arange(C), quarter * GROUPS + np.arange(C) // (C // GROUPS)] = 1.0
    return spread


def head_matrix():
    heads = np.arange(C) // HEAD_DIM
    return (heads[:, None] == heads[None, :]).astype(np.float32)


def head_rows():
    return (np.arange(HEADS)[:, None] == np.arange(C)[None, :] // HEAD_DIM).astype(np.float32)


def call(kernel, out_shape, *args, grid=None, in_specs=None, out_specs=None, flops=10**8):
    total = sum(a.size * a.dtype.itemsize for a in args)
    extra = {}
    if grid is not None:
        extra = dict(grid=grid, in_specs=in_specs, out_specs=out_specs)
    return pl.pallas_call(
        kernel,
        out_shape=out_shape,
        compiler_params=pltpu.CompilerParams(vmem_limit_bytes=56 * 2**20),
        cost_estimate=pl.CostEstimate(flops=flops, bytes_accessed=total, transcendentals=0),
        **extra,
    )(*args)


def image_sums(frames, sets, x_ref, t_ref, g_ref):
    cols = x_ref.shape[0]
    count = t_ref.shape[1] // frames
    first = jnp.zeros((count, frames, C), F32)
    cross = jnp.zeros((count, frames, C), F32)
    for w in range(cols):
        t = t_ref[w].astype(F32).reshape(count, frames, C)
        first = first + t
        cross = cross + t * x_ref[w][None]
    first = jnp.sum(first, axis=1)
    cross = jnp.sum(cross, axis=1)
    half = count // sets
    packed = jnp.zeros((half, 128), F32)
    for k in range(sets):
        part = slice(k * half, (k + 1) * half)
        packed = packed + hdot(first[part], g_ref[2 * k]) + hdot(cross[part], g_ref[2 * k + 1])
    return packed


MESH = pl.DeviceIdType.MESH


class Halo:
    def __init__(self, tile, tiles, sources, lows, highs, send_sem, recv_sem):
        self.tile, self.tiles = tile, tiles
        self.up, self.down = [], []
        for i, (source, low, high) in enumerate(zip(sources, lows, highs)):
            for copies, target, place, slot in (
                (self.up, low, lax.rem(tile + 1, tiles), 2 * i),
                (self.down, high, lax.rem(tile + tiles - 1, tiles), 2 * i + 1),
            ):
                copies.append(
                    pltpu.make_async_remote_copy(
                        src_ref=source,
                        dst_ref=target,
                        send_sem=send_sem.at[slot],
                        recv_sem=recv_sem.at[slot],
                        device_id={"tile": place},
                        device_id_type=MESH,
                    )
                )

    def start(self):
        @pl.when(self.tile < self.tiles - 1)
        def _():
            for copy in self.up:
                copy.start()

        @pl.when(self.tile > 0)
        def _():
            for copy in self.down:
                copy.start()

    def wait(self):
        @pl.when(self.tile < self.tiles - 1)
        def _():
            for copy in self.up:
                copy.wait_send()
            for copy in self.down:
                copy.wait_recv()

        @pl.when(self.tile > 0)
        def _():
            for copy in self.down:
                copy.wait_send()
            for copy in self.up:
                copy.wait_recv()


def tile_sends(tile, tiles, source, slots, send_sem, recv_sem):
    return [
        pltpu.make_async_remote_copy(
            src_ref=source,
            dst_ref=slots.at[tile],
            send_sem=send_sem.at[offset - 1],
            recv_sem=recv_sem.at[offset - 1],
            device_id={"tile": lax.rem(tile + offset, tiles)},
            device_id_type=MESH,
        )
        for offset in range(1, tiles)
    ]


def signal_peers(axis, me, count):
    barrier = pltpu.get_barrier_semaphore()
    for offset in range(1, count):
        pl.semaphore_signal(
            barrier, inc=1, device_id={axis: lax.rem(me + offset, count)}, device_id_type=MESH
        )


def add_slots(slots):
    total = slots[0]
    for i in range(1, slots.shape[0]):
        total = total + slots[i]
    return total


def input_kernel(
    frames,
    x_ref,
    t_ref,
    g_ref,
    out_ref,
    x_lo,
    x_hi,
    t_lo,
    t_hi,
    mine,
    slots,
    send_sem,
    recv_sem,
    halo_send,
    halo_recv,
):
    tiles, tile = lax.axis_size("tile"), lax.axis_index("tile")
    signal_peers("tile", tile, tiles)
    x = x_ref[...].reshape(-1, C)
    lat = jnp.broadcast_to(jnp.sum(x, axis=0, keepdims=True), (8, C))
    square = jnp.broadcast_to(jnp.sum(x * x, axis=0, keepdims=True), (8, C))
    mine[0:8] = hdot(lat, g_ref[0]) + hdot(square, g_ref[1])
    mine[8:] = image_sums(frames, 2, x_ref, t_ref, g_ref)
    slots[tile] = mine[...]
    pl.semaphore_wait(pltpu.get_barrier_semaphore(), tiles - 1)
    sketches = t_ref.at[:, : t_ref.shape[1] // 2]
    halo = Halo(tile, tiles, (x_ref, sketches), (x_lo, t_lo), (x_hi, t_hi), halo_send, halo_recv)
    sends = tile_sends(tile, tiles, mine, slots, send_sem, recv_sem)
    for copy in sends:
        copy.start()
    halo.start()
    for copy in sends:
        copy.wait()
    out_ref[...] = add_slots(slots)
    halo.wait()


def sketch_kernel(
    frames,
    own,
    x_ref,
    s_ref,
    t_ref,
    g_ref,
    out_ref,
    s_all,
    s_lo,
    s_hi,
    mine,
    slots,
    send_sem,
    recv_sem,
    halo_send,
    halo_recv,
    share_send,
    share_recv,
):
    tiles, tile = lax.axis_size("tile"), lax.axis_index("tile")
    shares, share = lax.axis_size("probe"), lax.axis_index("probe")
    signal_peers("tile", tile, tiles)
    signal_peers("probe", share, shares)
    s_all[0] = s_ref[:, : own * frames]
    pl.semaphore_wait(pltpu.get_barrier_semaphore(), tiles + shares - 2)
    source = s_ref if own * frames == s_ref.shape[1] else s_ref.at[:, : own * frames]
    gathers = [
        pltpu.make_async_remote_copy(
            src_ref=source,
            dst_ref=s_all.at[i],
            send_sem=share_send.at[i - 1],
            recv_sem=share_recv.at[i - 1],
            device_id={"probe": lax.rem(share + i, shares)},
            device_id_type=MESH,
        )
        for i in range(1, shares)
    ]
    for copy in gathers:
        copy.start()
    halo = Halo(tile, tiles, (s_ref,), (s_lo,), (s_hi,), halo_send, halo_recv)
    halo.start()
    packed = image_sums(frames, 1, x_ref, s_ref, g_ref)
    for copy in gathers:
        copy.wait()
    mine[...] = packed + pack_gram(frames, share, s_all, t_ref, packed.shape[0])
    slots[tile] = mine[...]
    sends = tile_sends(tile, tiles, mine, slots, send_sem, recv_sem)
    for copy in sends:
        copy.start()
    for copy in sends:
        copy.wait()
    out_ref[...] = add_slots(slots)
    halo.wait()


def reduce_kernel(axes, x_ref, out_ref, slots, send_sem, recv_sem):
    tiles, shares = lax.axis_size("tile"), lax.axis_size("probe")
    tile, share = lax.axis_index("tile"), lax.axis_index("probe")
    both = len(axes) == 2
    if both:
        count, me = tiles * shares, tile * shares + share
    elif axes[0] == "tile":
        count, me = tiles, tile
    else:
        count, me = shares, share

    def device(offset):
        other = lax.rem(me + offset, count)
        if both:
            return {"tile": other // shares, "probe": lax.rem(other, shares)}
        return {axes[0]: other}

    barrier = pltpu.get_barrier_semaphore()
    for offset in range(1, count):
        pl.semaphore_signal(
            barrier, inc=1, device_id=device(offset), device_id_type=pl.DeviceIdType.MESH
        )
    pl.semaphore_wait(barrier, count - 1)
    copies = []
    for offset in range(1, count):
        copy = pltpu.make_async_remote_copy(
            src_ref=x_ref,
            dst_ref=slots.at[me],
            send_sem=send_sem.at[offset - 1],
            recv_sem=recv_sem.at[offset - 1],
            device_id=device(offset),
            device_id_type=pl.DeviceIdType.MESH,
        )
        copy.start()
        copies.append(copy)
    slots[me] = x_ref[...]
    for copy in copies:
        copy.wait()
    total = slots[0]
    for i in range(1, count):
        total = total + slots[i]
    out_ref[...] = total


def reduce_over(array, axes, collective_id):
    count = math.prod(lax.axis_size(axis) for axis in axes)
    return pl.pallas_call(
        functools.partial(reduce_kernel, axes),
        out_shape=jax.ShapeDtypeStruct(array.shape, array.dtype),
        in_specs=[pl.BlockSpec(memory_space=pltpu.VMEM)],
        out_specs=pl.BlockSpec(memory_space=pltpu.VMEM),
        scratch_shapes=[
            pltpu.VMEM((count,) + array.shape, array.dtype),
            pltpu.SemaphoreType.DMA((count - 1,)),
            pltpu.SemaphoreType.DMA((count - 1,)),
        ],
        compiler_params=pltpu.CompilerParams(collective_id=collective_id, has_side_effects=True),
    )(array)


def latent_stats(ls_ref, members, gt_ref):
    sums = ls_ref[...]
    mean = hdot(sums, gt_ref[0])[0:1] / members
    inv = lax.rsqrt(hdot(sums, gt_ref[1])[0:1] / members - mean * mean + EPS)
    return mean, inv


def inside(r):
    tile = lax.axis_index("tile")
    return tile > 0 if r == 0 else tile < lax.axis_size("tile") - 1


def conv_rows(act, w_ref, cols, per):
    total = None
    left = None
    right = None
    span = cols * per
    for a in range(3):
        mid = dot(act[a], w_ref[3 * a + 1])
        lo = dot(act[a][: span - per], w_ref[3 * a])
        hi = dot(act[a][per:], w_ref[3 * a + 2])
        total = mid if total is None else total + mid
        left = lo if left is None else left + lo
        right = hi if right is None else right + hi
    zero = jnp.zeros((per, C), F32)
    return (
        total + jnp.concatenate([zero, left], axis=0) + jnp.concatenate([right, zero], axis=0)
    )


def conv_frames(signal, w_ref, frames):
    rows = signal.shape[0]
    place = lax.rem(iota((rows, C), 0), frames)
    before = pltpu.roll(dot(signal, w_ref[0]), 1, 0)
    after = pltpu.roll(dot(signal, w_ref[2]), rows - 1, 0)
    return (
        dot(signal, w_ref[1])
        + jnp.where(place > 0, before, 0.0)
        + jnp.where(place < frames - 1, after, 0.0)
    )


def primal_kernel(
    members,
    temper_ref,
    lo_ref,
    x_ref,
    hi_ref,
    ls_ref,
    vec_ref,
    ws_ref,
    wt_ref,
    wqkv_ref,
    wo_ref,
    gt_ref,
    hh_ref,
    out_ref,
    a_ref,
    b_ref,
    qk_ref,
    kexp_ref,
    qexp_ref,
    vexp_ref,
    w_ref,
    wbd_ref,
):
    cols, frames = x_ref.shape[0], x_ref.shape[1]
    rows = cols * frames
    hf = HEADS * frames
    mean, inv = latent_stats(ls_ref, members, gt_ref)
    gain = vec_ref[0:1]
    acts = []
    for r, ref in enumerate((lo_ref, x_ref, hi_ref)):
        value = ref[...].reshape(rows, C)
        if r != 1:
            value = jnp.where(inside(r), value, 0.0)
        centered = value - mean
        normed = centered * inv * gain + vec_ref[1:2]
        sig = jax.nn.sigmoid(normed)
        slope = sig * (1.0 + normed * (1.0 - sig)) * gain
        active = normed * sig
        if r != 1:
            keep = jnp.where(inside(r), 1.0, 0.0)
            slope = slope * keep
            active = active * keep
        a_ref[r] = (slope * inv).reshape(cols, frames, C)
        b_ref[r] = (slope * centered).reshape(cols, frames, C)
        acts.append(active.astype(BF16))
    spatial = (conv_rows(acts, ws_ref, cols, frames) + vec_ref[2:3]).astype(BF16)
    residual = x_ref[...].reshape(rows, C) + vec_ref[3:4] + conv_frames(spatial, wt_ref, frames)
    rounded = residual.astype(BF16)
    q = dot(rounded, wqkv_ref[0])
    k = dot(rounded, wqkv_ref[1])
    v = dot(rounded, wqkv_ref[2])
    hh = hh_ref[...]
    rq = 1.0 / jnp.sqrt(hdot(q * q, hh) / HEAD_DIM + 1.0)
    rk = 1.0 / jnp.sqrt(hdot(k * k, hh) / HEAD_DIM + 1.0)
    shape = (cols, frames, C)
    qk_ref[0] = q.reshape(shape)
    qk_ref[1] = (q * rq * rq * rq).reshape(shape)
    qk_ref[2] = rq.reshape(shape)
    qk_ref[3] = k.reshape(shape)
    qk_ref[4] = (k * rk * rk * rk).reshape(shape)
    qk_ref[5] = rk.reshape(shape)
    qu = q * rq
    ku = k * rk
    head_of_row = iota((hf, C), 0) // frames
    channel = iota((hf, C), 1)
    mask = jnp.where(
        (channel >= head_of_row * HEAD_DIM) & (channel < (head_of_row + 1) * HEAD_DIM), 1.0, 0.0
    )
    scale = jnp.zeros((hf, C), F32)
    for h in range(HEADS):
        scale = jnp.where(head_of_row == h, temper_ref[h] / math.sqrt(HEAD_DIM), scale)
    scale = scale * mask
    segment = jnp.where(same_block(hf, hf, frames), 1.0, 0.0)
    ei = iota((hf, HEADS * hf), 0)
    ej = iota((hf, HEADS * hf), 1)
    spread = jnp.where(
        (ei // frames == ej // hf) & (lax.rem(ei, frames) == lax.rem(ej, frames)), 1.0, 0.0
    ).astype(BF16)
    di = iota((hf, HEADS * hf), 0) // frames
    dj = lax.rem(ej, hf) // frames
    diagonal = jnp.where(di == dj, 1.0, 0.0)
    mixes = []
    for w in range(cols):
        part = slice(w * frames, (w + 1) * frames)
        k_rows = jnp.concatenate([ku[part]] * HEADS, axis=0) * scale
        q_rows = jnp.concatenate([qu[part]] * HEADS, axis=0) * scale
        v_rows = jnp.concatenate([v[part]] * HEADS, axis=0) * mask
        kexp_ref[w] = k_rows.astype(BF16)
        qexp_ref[w] = q_rows.astype(BF16)
        vexp_ref[w] = v_rows.astype(BF16)
        exponent = jnp.exp(ndot(qu[part], k_rows, HIGHEST))
        weights = exponent / hdot(exponent, segment)
        w_ref[w] = weights
        mixes.append(hdot(weights, v_rows))
        wide = dot(weights.astype(BF16), spread)
        wbd_ref[w] = (jnp.concatenate([wide] * CHUNK, axis=0) * diagonal).astype(BF16)
    mixture = jnp.concatenate(mixes, axis=0).astype(BF16)
    out_ref[...] = (residual + dot(mixture, wo_ref[...])).astype(BF16).reshape(shape)


def tangent_kernel(
    members,
    which,
    lo_ref,
    t_ref,
    hi_ref,
    sums_ref,
    ls_ref,
    ws_ref,
    wt_ref,
    wqkv_ref,
    wo_ref,
    gt_ref,
    hh_ref,
    hrow_ref,
    a_ref,
    b_ref,
    qk_ref,
    kexp_ref,
    qexp_ref,
    vexp_ref,
    w_ref,
    wbd_ref,
    out_ref,
):
    cols, frames = a_ref.shape[1], a_ref.shape[2]
    per = CHUNK * frames
    hf = HEADS * frames
    mean, inv = latent_stats(ls_ref, members, gt_ref)
    first = hdot(sums_ref[...], gt_ref[2 * which])
    cross = hdot(sums_ref[...], gt_ref[2 * which + 1])
    d_mean = (first / members)[:, None, :]
    d_var = 2.0 * (cross - mean * first) / members
    d_std = (-0.5 * inv * inv * inv * d_var)[:, None, :]
    acts = []
    for r, ref in enumerate((lo_ref, t_ref, hi_ref)):
        pieces = []
        for w in range(cols):
            t = ref[w].astype(F32).reshape(CHUNK, frames, C)
            if r != 1:
                t = jnp.where(inside(r), t, 0.0)
            piece = a_ref[r, w][None] * (t - d_mean) + b_ref[r, w][None] * d_std
            pieces.append(piece.reshape(per, C).astype(BF16))
        acts.append(jnp.concatenate(pieces, axis=0))
    spatial = conv_rows(acts, ws_ref, cols, per).astype(BF16)
    residual = t_ref[...].reshape(cols * per, C).astype(F32) + conv_frames(spatial, wt_ref, frames)
    rounded = residual.astype(BF16)
    shape = (cols, CHUNK, frames, C)
    hh = hh_ref[...].astype(BF16)

    def unit_shift(base, projection):
        value, cube, inverse = (qk_ref[base + i][:, None] for i in range(3))
        moved = dot(rounded, projection).reshape(shape)
        along = dot((value * moved).reshape(cols * per, C).astype(BF16), hh) * (1.0 / HEAD_DIM)
        return (moved * inverse - cube * along.reshape(shape)).reshape(cols * per, C).astype(BF16)

    dqu = unit_shift(0, wqkv_ref[0])
    dku = unit_shift(3, wqkv_ref[1])
    dv = dot(rounded, wqkv_ref[2])
    on_diagonal = same_block(hf, per, frames)
    segment = jnp.where(same_block(hf, hf, frames), 1.0, 0.0).astype(BF16)
    mixes = []
    for w in range(cols):
        part = slice(w * per, (w + 1) * per)
        scores = ndot(dqu[part], kexp_ref[w])
        turned = ndot(qexp_ref[w], dku[part])
        for d in range(HEADS):
            moved = pltpu.roll(turned, d * frames, 1) if d else turned
            moved = jnp.where(on_diagonal, moved, 0.0)
            if d:
                moved = jnp.concatenate([moved[d * frames :], moved[: d * frames]], axis=0)
            scores = scores + moved
        weights = jnp.concatenate([w_ref[w]] * CHUNK, axis=0)
        weighted = weights * scores
        top = weighted.astype(BF16)
        rest = (weighted - top.astype(F32)).astype(BF16)
        shift = weighted - weights * (dot(top, segment) + dot(rest, segment))
        own = dv[part]
        heads = [(own * hrow_ref[h : h + 1]).astype(BF16) for h in range(HEADS)]
        mix = dot(shift.astype(BF16), vexp_ref[w]) + dot(
            wbd_ref[w], jnp.concatenate(heads, axis=0)
        )
        mixes.append(mix.astype(BF16))
    result = residual + dot(jnp.concatenate(mixes, axis=0), wo_ref[...])
    out_ref[...] = result.reshape(cols, per, C).astype(out_ref.dtype)


def gather_rows(ref, w, share):
    count = ref.shape[0]
    return jnp.concatenate(
        [ref[lax.rem(share - p + count, count), w] for p in range(count)], axis=0
    )


def pack_gram(frames, share, s_ref, t_ref, own):
    cols = t_ref.shape[0]
    half = t_ref.shape[1] // 2
    total = None
    for w in range(cols):
        s = gather_rows(s_ref, w, share)
        term = ndot(jnp.concatenate([s, t_ref[w, half:]], axis=0), s)
        total = term if total is None else total + term
    rows, columns = total.shape
    same = lax.rem(iota((rows, columns), 0), frames) == lax.rem(iota((rows, columns), 1), frames)
    total = jnp.where(same, total, 0.0)
    summed = jnp.sum(total.reshape(rows // frames, frames, columns), axis=1)
    ns = columns // frames
    packed = jnp.zeros((own, 128), F32)
    for i in range(rows // frames // own):
        fold = jnp.where(
            iota((columns, 128), 0) // frames + (64 + i * ns) == iota((columns, 128), 1), 1.0, 0.0
        )
        packed = packed + hdot(summed[i * own : (i + 1) * own], fold)
    return packed


def combine_kernel(
    frames, ns, count, total, gram_ref, s_ref, js_ref, t_ref, jt_ref, basis_ref, bi_ref, ti_ref, f_ref
):
    cols = t_ref.shape[0]
    own = gram_ref.shape[0]
    packed = gram_ref[...]
    pieces = []
    for i in range(ns // own + 1):
        choose = jnp.where(iota((128, ns), 0) == iota((128, ns), 1) + (64 + i * ns), 1.0, 0.0)
        pieces.append(hdot(packed, choose))
    gram = jnp.concatenate(pieces[:-1], axis=0)
    cross = pieces[-1]
    inverse = jnp.where(iota((ns, ns), 0) == iota((ns, ns), 1), 1.0, 0.0)
    row = iota((ns, ns), 0)
    for j in range(ns):
        scale = 1.0 / jnp.sqrt(gram[j : j + 1, j : j + 1])
        column = gram[:, j : j + 1] * scale
        upper = gram[j : j + 1, :] * scale
        lower = inverse[j : j + 1, :] * scale
        gram = jnp.where(row > j, gram - column * upper, gram)
        inverse = jnp.where(row > j, inverse - column * lower, jnp.where(row == j, lower, inverse))
    share = lax.axis_index("probe")
    first = share * count
    pick = jnp.where(iota((own, ns), 1) == iota((own, ns), 0) + first, 1.0, 0.0)
    to_basis = math.sqrt(total) * hdot(pick, inverse)
    to_project = hdot(ndot(cross, inverse, HIGHEST), inverse)
    big, wide = own * frames, ns * frames
    spread_rows = jnp.where(iota((big, own), 0) // frames == iota((big, own), 1), 1.0, 0.0)
    spread_columns = jnp.where(iota((ns, wide), 1) // frames == iota((ns, wide), 0), 1.0, 0.0)
    same = lax.rem(iota((big, wide), 0), frames) == lax.rem(iota((big, wide), 1), frames)

    def expand(matrix):
        full = jnp.where(same, hdot(spread_rows, hdot(matrix, spread_columns)), 0.0)
        parts = []
        for _ in range(3):
            piece = full.astype(BF16)
            parts.append(piece)
            full = full - piece.astype(F32)
        return parts

    basis_parts = expand(to_basis)
    project_parts = expand(to_project)

    def apply(parts, array):
        result = dot(parts[0], array)
        for piece in parts[1:]:
            result = result + dot(piece, array)
        return result

    sums = [jnp.zeros((big, C), F32) for _ in range(3)]
    for w in range(cols):
        s = gather_rows(s_ref, w, share)
        js = gather_rows(js_ref, w, share)
        basis = apply(basis_parts, s)
        projected = t_ref[w, t_ref.shape[1] // 2 :].astype(F32) - apply(project_parts, s)
        basis_image = apply(basis_parts[:2], js)
        test_image = jt_ref[w] - apply(project_parts[:2], js)
        basis_ref[w] = basis
        bi_ref[w] = basis_image.astype(BF16)
        ti_ref[w] = test_image.astype(BF16)
        sums[0] = sums[0] + basis * basis_image
        sums[1] = sums[1] + projected * test_image
        sums[2] = sums[2] + projected * projected
    lane = iota((own, 128), 1)
    forms = jnp.zeros((own, 128), F32)
    for i in range(3):
        value = jnp.sum(jnp.sum(sums[i].reshape(own, frames, C), axis=1), axis=1, keepdims=True)
        forms = jnp.where(lane == 4 * share + i, value, forms)
    f_ref[...] = forms


def on_device(
    latent,
    probes,
    gn_gain,
    gn_bias,
    w_spatial,
    spatial_bias,
    w_temporal,
    temporal_bias,
    w_qkv,
    w_out,
    temper,
):
    frames, cols = latent.shape[0], latent.shape[2]
    own = probes.shape[1]
    tiles, shares = lax.axis_size("tile"), lax.axis_size("probe")
    ns = own * shares
    padded = -(-own // CHUNK) * CHUNK
    total = latent.size * tiles
    members = total // GROUPS
    hf = HEADS * frames

    x = jnp.swapaxes(latent[:, 0], 0, 1)
    p = jnp.transpose(probes[:, :, :, 0], (3, 0, 1, 2, 4))
    if padded != own:
        p = jnp.pad(p, ((0, 0), (0, 0), (0, padded - own), (0, 0), (0, 0)))
    p = p.reshape(cols, 2 * padded * frames, C)
    group = jnp.asarray(group_matrix())
    group_t = jnp.asarray(np.swapaxes(group_matrix(), 1, 2))
    hh = jnp.asarray(head_matrix())
    hrow = jnp.asarray(head_rows())
    smem = pl.BlockSpec(memory_space=pltpu.SMEM)
    vmem = pl.BlockSpec(memory_space=pltpu.VMEM)
    anywhere = pl.BlockSpec(memory_space=pl.ANY)

    def like(array):
        return jax.ShapeDtypeStruct(array.shape, array.dtype)

    def exchange(kernel, args, outs, out_specs, rows, halos, collective_id, extra=()):
        block = (rows, 128)
        semaphores = pltpu.SemaphoreType.DMA
        return pl.pallas_call(
            kernel,
            in_specs=[vmem] * len(args),
            out_shape=[jax.ShapeDtypeStruct(block, F32)] + outs,
            out_specs=[vmem] + out_specs,
            scratch_shapes=[
                pltpu.VMEM(block, F32),
                pltpu.VMEM((tiles,) + block, F32),
                semaphores((tiles - 1,)),
                semaphores((tiles - 1,)),
                semaphores((2 * halos,)),
                semaphores((2 * halos,)),
            ]
            + [semaphores(shape) for shape in extra],
            compiler_params=pltpu.CompilerParams(
                collective_id=collective_id,
                has_side_effects=True,
                vmem_limit_bytes=40 * 2**20,
            ),
        )(*args)

    half = jax.ShapeDtypeStruct((cols, padded * frames, C), BF16)
    sums, x_lo, x_hi, p_lo, p_hi = exchange(
        functools.partial(input_kernel, frames),
        (x, p, group),
        [like(x), like(x), half, half],
        [anywhere] * 4,
        8 + padded,
        2,
        0,
    )
    latent_sums, probe_sums = sums[:8], sums[8:]
    tests, _ = lax.optimization_barrier((p[:, padded * frames :], sums))
    forward = [(i, i + 1) for i in range(tiles - 1)]
    test_lo = lax.ppermute(tests, "tile", forward)
    test_hi = lax.ppermute(tests, "tile", [(j, i) for i, j in forward])
    wqkv = jnp.swapaxes(w_qkv, 0, 1)
    primal = pl.pallas_call(
        functools.partial(primal_kernel, members),
        in_specs=[smem] + [vmem] * 11,
        out_shape=[
            jax.ShapeDtypeStruct((cols, frames, C), BF16),
            jax.ShapeDtypeStruct((3, cols, frames, C), F32),
            jax.ShapeDtypeStruct((3, cols, frames, C), F32),
            jax.ShapeDtypeStruct((6, cols, frames, C), F32),
            jax.ShapeDtypeStruct((cols, hf, C), BF16),
            jax.ShapeDtypeStruct((cols, hf, C), BF16),
            jax.ShapeDtypeStruct((cols, hf, C), BF16),
            jax.ShapeDtypeStruct((cols, frames, hf), F32),
            jax.ShapeDtypeStruct((cols, hf, HEADS * hf), BF16),
        ],
        compiler_params=pltpu.CompilerParams(vmem_limit_bytes=56 * 2**20),
        cost_estimate=pl.CostEstimate(flops=10**8, bytes_accessed=10**7, transcendentals=0),
    )(
        temper,
        x_lo,
        x,
        x_hi,
        latent_sums,
        jnp.stack([gn_gain, gn_bias, spatial_bias, temporal_bias]),
        w_spatial,
        w_temporal,
        wqkv,
        w_out,
        group_t,
        hh,
    )
    block_out, caches = primal[0], primal[1:]
    chunks = padded // CHUNK
    per = CHUNK * frames

    def tangent(lo, mid, hi, offset, sums, which, dtype):
        fixed = (latent_sums, w_spatial, w_temporal, wqkv, w_out, group_t, hh, hrow) + tuple(caches)
        moving = pl.BlockSpec((cols, per, C), lambda i: (0, i + offset, 0))
        side = pl.BlockSpec((cols, per, C), lambda i: (0, i, 0))
        stat = pl.BlockSpec((CHUNK, 128), lambda i: (i, 0))
        return call(
            functools.partial(tangent_kernel, members, which),
            jax.ShapeDtypeStruct((cols, padded * frames, C), dtype),
            lo,
            mid,
            hi,
            sums,
            *fixed,
            grid=(chunks,),
            in_specs=[side, moving, side, stat] + [vmem] * len(fixed),
            out_specs=pl.BlockSpec((cols, per, C), lambda i: (0, i, 0)),
            flops=2 * 10**9,
        )

    def from_shares(block):
        blocks = [block]
        for i in range(1, shares):
            ring = [(j, (j + i) % shares) for j in range(shares)]
            blocks.append(lax.ppermute(block, "probe", ring))
        return jnp.stack(blocks)

    sketch = tangent(p_lo, p, p_hi, 0, probe_sums, 0, BF16)
    gram, s_all, s_lo, s_hi = exchange(
        functools.partial(sketch_kernel, frames, own),
        (x, sketch, p, group),
        [jax.ShapeDtypeStruct((shares, cols, own * frames, C), BF16), like(sketch), like(sketch)],
        [vmem, anywhere, anywhere],
        padded,
        1,
        1,
        [(shares - 1,), (shares - 1,)],
    )
    test = tangent(test_lo, p, test_hi, chunks, probe_sums, 1, F32)
    second = tangent(s_lo, sketch, s_hi, 0, gram, 0, BF16)
    js_all = from_shares(second[:, : own * frames])
    image = (cols, padded * frames, C)
    basis, basis_images, test_images, forms = pl.pallas_call(
        functools.partial(combine_kernel, frames, ns, own, total),
        in_specs=[vmem] * 5,
        out_shape=[
            jax.ShapeDtypeStruct(image, F32),
            jax.ShapeDtypeStruct(image, BF16),
            jax.ShapeDtypeStruct(image, BF16),
            jax.ShapeDtypeStruct((padded, 128), F32),
        ],
        compiler_params=pltpu.CompilerParams(vmem_limit_bytes=56 * 2**20),
        cost_estimate=pl.CostEstimate(flops=10**9, bytes_accessed=10**7, transcendentals=0),
    )(gram, s_all, js_all, p, test)

    if tiles * shares <= 64:
        forms = reduce_over(forms, ("tile", "probe"), 2)
    else:
        forms = reduce_over(reduce_over(forms, ("tile",), 2), ("probe",), 3)
    placed = jnp.transpose(forms[:own, : 4 * shares].reshape(own, shares, 4), (2, 1, 0))
    placed = placed.reshape(4, ns)
    rayleigh = jnp.stack([placed[0] / total, placed[1] / placed[2]])
    divergence = (jnp.sum(placed[0]) / total + jnp.sum(placed[1]) / ns) / total

    def restore(array):
        array = array.reshape(cols, padded, frames, C)[:, :own]
        return jnp.transpose(array, (1, 2, 0, 3))[:, :, None]

    return (
        jnp.swapaxes(block_out, 0, 1)[:, None],
        restore(basis),
        restore(basis_images),
        restore(test_images),
        rayleigh,
        divergence,
    )


def solution(mesh):
    in_specs = (
        P(None, "tile", None, None),
        P(None, "probe", None, "tile", None, None),
        P(),
        P(),
        P(),
        P(),
        P(),
        P(),
        P(),
        P(),
        P(),
    )
    out_specs = (
        P(None, "tile", None, None),
        P("probe", None, "tile", None, None),
        P("probe", None, "tile", None, None),
        P("probe", None, "tile", None, None),
        P(),
        P(),
    )
    return jax.shard_map(
        on_device, mesh=mesh, in_specs=in_specs, out_specs=out_specs, check_vma=False
    )
```
